1024 devices in a mesh: grp: 2 (over z_lo), ta: 8 (over y), xyz: 64 (over z_hi, x, core).
Axes of the slice: x: 8, y: 8, z: 8 (z_hi: 4, z_lo: 2; z = z_hi * 2 + z_lo), core: 2. Of those that a mesh axis runs over, the one named last changes fastest.
Arguments:
- links: float32 [4, 3, 3, 2, 16, 64, 256], P(None, None, None, None, ('grp', 'ta'), 'xyz'), may hold values from -1 to 1, as said below
- momenta: float32 [4, 3, 3, 2, 16, 64, 256], P(None, None, None, None, ('grp', 'ta'), 'xyz'), may hold values from -11 to 11, as said below
- vectors: float32 [16, 3, 2, 2, 8, 64, 256], P('grp', None, None, None, 'ta', 'xyz'), may hold values from -6 to 6
- coefficients: float32 [4], replicated, may hold values from -1 to 1
Outputs:
- new_links: float32 [4, 3, 3, 2, 16, 64, 256], P(None, None, None, None, ('grp', 'ta'), 'xyz')
- new_momenta: float32 [4, 3, 3, 2, 16, 64, 256], P(None, None, None, None, ('grp', 'ta'), 'xyz')
- filtered: float32 [16, 3, 2, 2, 8, 64, 256], P('grp', None, None, None, 'ta', 'xyz')
The draws below stay inside these ranges and needn't reach their ends.
Inputs may be any that keep to these rules, and one draw needn't show every extreme that they name: `links`: every 3 x 3 link matrix is special unitary up to rounding. `momenta`: every 3 x 3 momentum matrix is anti-Hermitian and traceless: an entry below the diagonal has exactly the negated real part and the same imaginary part as its mirror above, the diagonal has zero real parts.
All inputs are finite; a program needn't handle non-finite values.
Results may differ from the reference program's by a relative error of at most 0.0001.
Values sent between devices are 32-bit elements; how exact they have to be, the bound alone decides.
No kernel may reach another device: no remote copies, remote signals or barrier semaphores. Data moves between devices by JAX's collectives and lax.ppermute only.
A program may use at most 64 MiB of HBM per device.

```python
import jax
import jax.numpy as jnp
from jax import lax

NV = 16
NY = 8
NZ = 32
NSTEP = 2
NCHEB = 3
NT = 16
NHALF = 8
NX = 64


def conjugate_inner(left_side, right_side):
    real_part = jnp.sum(left_side[:, :, 0] * right_side[:, :, 0] + left_side[:, :, 1] * right_side[:, :, 1], axis=1)
    imag_part = jnp.sum(left_side[:, :, 0] * right_side[:, :, 1] - left_side[:, :, 1] * right_side[:, :, 0], axis=1)
    return (real_part, imag_part)


def draw_links(key, part):
    shape_sites = (NT, NX, NY * NZ)
    sample = jax.random.normal(key, (2, 4, 3, 2) + shape_sites, jnp.float32)
    row_one = sample[0]
    row_one = row_one / jnp.sqrt(jnp.sum(row_one * row_one, axis=(1, 2)))[:, None, None]
    correlation_re, correlation_im = conjugate_inner(row_one, sample[1])
    second_re = sample[1][:, :, 0] - (correlation_re[:, None] * row_one[:, :, 0] - correlation_im[:, None] * row_one[:, :, 1])
    second_im = sample[1][:, :, 1] - (correlation_re[:, None] * row_one[:, :, 1] + correlation_im[:, None] * row_one[:, :, 0])
    row_two = jnp.stack([second_re, second_im], axis=2)
    row_two = row_two / jnp.sqrt(jnp.sum(row_two * row_two, axis=(1, 2)))[:, None, None]
    one_re = row_one[:, :, 0]
    one_im = row_one[:, :, 1]
    two_re = row_two[:, :, 0]
    two_im = row_two[:, :, 1]
    pieces = []
    for colour in range(3):
        second_col = (colour + 1) % 3
        third_col = (colour + 2) % 3
        cross_re = one_re[:, second_col] * two_re[:, third_col] - one_im[:, second_col] * two_im[:, third_col] - (one_re[:, third_col] * two_re[:, second_col] - one_im[:, third_col] * two_im[:, second_col])
        cross_im = one_re[:, second_col] * two_im[:, third_col] + one_im[:, second_col] * two_re[:, third_col] - (one_re[:, third_col] * two_im[:, second_col] + one_im[:, third_col] * two_re[:, second_col])
        pieces.append(jnp.stack([cross_re, -cross_im], axis=1))
    row_three = jnp.stack(pieces, axis=1)
    generic = jnp.stack([row_one, row_two, row_three], axis=1)
    plant_key = jax.random.fold_in(key, 7)
    phase_key = jax.random.fold_in(key, 11)
    planted = jax.random.randint(plant_key, (4,) + shape_sites, 0, 16) == 0
    phases = jax.random.uniform(phase_key, (2, 4) + shape_sites, jnp.float32, -jnp.pi, jnp.pi)
    angles = jnp.stack([phases[0], phases[1], -(phases[0] + phases[1])], axis=1)
    unit_eye = jnp.eye(3, dtype=jnp.float32).reshape(1, 3, 3, 1, 1, 1)
    phase_re = unit_eye * jnp.cos(angles)[:, :, None]
    phase_im = unit_eye * jnp.sin(angles)[:, :, None]
    phase_matrix = jnp.stack([phase_re, phase_im], axis=3)
    return jnp.where(planted[:, None, None, None], phase_matrix, generic)


def draw_momenta(key, part):
    shape_all = (4, 3, 3, 2, NT, NX, NY * NZ)
    sample = jnp.clip(jax.random.normal(key, shape_all, jnp.float32), -4.0, 4.0)
    real_part = (sample[:, :, :, 0] - jnp.swapaxes(sample[:, :, :, 0], 1, 2)) * 0.5
    imag_part = (sample[:, :, :, 1] + jnp.swapaxes(sample[:, :, :, 1], 1, 2)) * 0.5
    diagonal = (imag_part[:, 0, 0] + imag_part[:, 1, 1] + imag_part[:, 2, 2]) / 3.0
    unit_eye = jnp.eye(3, dtype=jnp.float32).reshape(1, 3, 3, 1, 1, 1)
    imag_part = imag_part - unit_eye * diagonal[:, None, None]
    return jnp.stack([real_part, imag_part], axis=3)


def steps_of(own_key, extent, split, smallest, top_value):
    def one(position, parts):
        steps = jax.random.uniform(jax.random.fold_in(jax.random.fold_in(own_key, 6), position), (parts,), jnp.float32, smallest / len(split), top_value / len(split))
        return jnp.repeat(jnp.exp(steps), extent[position] // parts).reshape((-1,) + (1,) * (len(extent) - position - 1))

    gain = one(*split[0])
    for cut in split[1:]:
        gain = gain * one(*cut)
    return gain


def centred(own_key, shape, scale, bound, cuts=(), held_as=jnp.bfloat16):
    factor_of = steps_of(own_key, shape, cuts, -0.22, 0.18) if cuts else 1.0
    drawn = jax.random.normal(own_key, shape, jnp.float32) * scale * factor_of
    return jnp.minimum(jnp.maximum(drawn, -bound), bound).astype(held_as)


def setup_inputs(seed: int = 0) -> dict:
    splits = jax.random.split(jax.random.key(seed), 5)
    return {
        "links": draw_links(jax.random.fold_in(splits[4], 71), 0),
        "momenta": draw_momenta(jax.random.fold_in(splits[4], 71), 0),
        "vectors": centred(splits[2], (NV, 3, 2, 2, NHALF, NX, NY * NZ), 1.0, 6.0, ((0, 2), (4, 8), (5, 64)), jnp.float32),
        "coefficients": jnp.clip(jax.random.uniform(splits[3], (NCHEB + 1,), jnp.float32, -1.0, 1.0), -1.0, 1.0),
    }


coupling = 5.7
time_step = 0.1
taylor_degree = 6


def matrix_product(left_side, right_side):
    left_re = left_side[:, :, 0]
    left_im = left_side[:, :, 1]
    right_re = right_side[:, :, 0]
    right_im = right_side[:, :, 1]
    real_part = jnp.sum(left_re[:, :, None] * right_re[None] - left_im[:, :, None] * right_im[None], axis=1)
    imag_part = jnp.sum(left_re[:, :, None] * right_im[None] + left_im[:, :, None] * right_re[None], axis=1)
    return jnp.stack([real_part, imag_part], axis=2)


def hermitian_transpose(color_matrix):
    return jnp.stack([jnp.swapaxes(color_matrix[:, :, 0], 0, 1), -jnp.swapaxes(color_matrix[:, :, 1], 0, 1)], axis=2)


def identity_like(color_matrix):
    unit_eye = jnp.eye(3, dtype=jnp.float32).reshape((3, 3) + (1,) * (color_matrix.ndim - 3))
    real_part = jnp.broadcast_to(unit_eye, color_matrix[:, :, 0].shape)
    return jnp.stack([real_part, jnp.zeros_like(real_part)], axis=2)


def traceless_part(color_matrix):
    skew_part = (color_matrix - hermitian_transpose(color_matrix)) * 0.5
    trace_im = (skew_part[0, 0, 1] + skew_part[1, 1, 1] + skew_part[2, 2, 1]) / 3.0
    unit_eye = jnp.eye(3, dtype=jnp.float32).reshape((3, 3) + (1,) * trace_im.ndim)
    return jnp.stack([skew_part[:, :, 0], skew_part[:, :, 1] - unit_eye * trace_im], axis=2)


def taylor_exp(generator):
    identity = identity_like(generator)
    result = identity
    for degree in range(taylor_degree, 0, -1):
        result = identity + matrix_product(generator, result) / degree
    return result


def shift_lattice(entry_values, direction, amount):
    return jnp.roll(entry_values, -amount, axis=entry_values.ndim - 4 + direction)


def gauge_force(lattice):
    forces = []
    for direction in range(4):
        staple = jnp.zeros_like(lattice[0])
        for across in range(4):
            if across == direction:
                continue
            up_part = matrix_product(matrix_product(shift_lattice(lattice[across], direction, 1), hermitian_transpose(shift_lattice(lattice[direction], across, 1))), hermitian_transpose(lattice[across]))
            low_part = matrix_product(matrix_product(hermitian_transpose(shift_lattice(shift_lattice(lattice[across], direction, 1), across, -1)), hermitian_transpose(shift_lattice(lattice[direction], across, -1))), shift_lattice(lattice[across], across, -1))
            staple = staple + up_part
            staple = staple + low_part
        forces.append((coupling / 3.0) * traceless_part(matrix_product(lattice[direction], staple)))
    return jnp.stack(forces)


def multiply_by_matrix(color_matrix, entry_values):
    matrix_re = color_matrix[:, :, 0][None]
    matrix_im = color_matrix[:, :, 1][None]
    values_re = entry_values[:, :, 0][:, None]
    values_im = entry_values[:, :, 1][:, None]
    real_part = jnp.sum(matrix_re * values_re - matrix_im * values_im, axis=2)
    imag_part = jnp.sum(matrix_re * values_im + matrix_im * values_re, axis=2)
    return jnp.stack([real_part, imag_part], axis=2)


def hopping(spatial, entry_values):
    summand_terms = []
    for lattice_direction in range(3):
        color_matrix = spatial[lattice_direction]
        summand_terms.append(multiply_by_matrix(color_matrix, shift_lattice(entry_values, lattice_direction + 1, 1)))
        summand_terms.append(multiply_by_matrix(hermitian_transpose(shift_lattice(color_matrix, lattice_direction + 1, -1)), shift_lattice(entry_values, lattice_direction + 1, -1)))
    running_total = summand_terms[0]
    for summand_term in summand_terms[1:]:
        running_total = running_total + summand_term
    return running_total


def chebyshev(spatial, entry_values, coefficients):
    previous = entry_values
    current = hopping(spatial, entry_values) * (-1.0 / 6.0)
    result = coefficients[0] * previous
    result = result + coefficients[1] * current
    for degree in range(2, NCHEB + 1):
        following = 2.0 * (hopping(spatial, current) * (-1.0 / 6.0)) - previous
        result = result + coefficients[degree] * following
        previous = current
        current = following
    return result


def reference(links, momenta, vectors, coefficients):
    shape_links = links.shape
    batched_exp = jax.vmap(taylor_exp)
    batched_product = jax.vmap(matrix_product)
    lattice = links.reshape(4, 3, 3, 2, NT, NX, NY, NZ)
    moment = momenta.reshape(4, 3, 3, 2, NT, NX, NY, NZ)
    force_field = gauge_force(lattice)
    moment = moment - (0.5 * time_step) * force_field
    for counter in range(NSTEP):
        lattice = batched_product(batched_exp(time_step * moment), lattice)
        force_field = gauge_force(lattice)
        if counter + 1 < NSTEP:
            moment = moment - time_step * force_field
        else:
            moment = moment - (0.5 * time_step) * force_field
    spatial = [lattice[1], lattice[2], lattice[3]]
    fields = vectors.reshape(NV, 3, 2, NT, NX, NY, NZ)

    def filter_one(entry_values):
        return chebyshev(spatial, entry_values[None], coefficients)[0]

    filtered = lax.map(filter_one, fields)
    return lattice.reshape(shape_links), moment.reshape(shape_links), filtered.reshape(vectors.shape)
```

```python
import functools

import jax
import jax.numpy as jnp
from jax import lax
from jax.experimental import pallas as pl
from jax.experimental.pallas import tpu as pltpu
from jax.sharding import PartitionSpec as P

NZ = 32
NSTEP = 2
NCHEB = 3
coupling = 5.7
time_step = 0.1
taylor_degree = 6

AXES = ("grp", "ta", "xyz")
TILE = (8, 128)
F32 = jnp.float32


def roll(value, shift, axis):
    return pltpu.roll(value, shift % value.shape[axis], axis)


def iotas():
    row = lax.broadcasted_iota(jnp.int32, TILE, 0)
    lane = lax.broadcasted_iota(jnp.int32, TILE, 1)
    return row, lane


def load_matrix(entry):
    return [[(entry((i * 3 + j) * 2), entry((i * 3 + j) * 2 + 1)) for j in range(3)] for i in range(3)]


def product(left, right, left_h=False, right_h=False):
    out = []
    for i in range(3):
        line = []
        for j in range(3):
            real, imag = None, None
            for k in range(3):
                ar, ai = left[k][i] if left_h else left[i][k]
                br, bi = right[j][k] if right_h else right[k][j]
                rr, ii, ri, ir = ar * br, ai * bi, ar * bi, ai * br
                re = rr + ii if left_h != right_h else rr - ii
                if left_h and right_h:
                    im_terms = (-1, ri, ir)
                elif left_h:
                    im_terms = (1, ri, -1, ir)
                elif right_h:
                    im_terms = (1, ir, -1, ri)
                else:
                    im_terms = (1, ri, ir)
                real = re if real is None else real + re
                if len(im_terms) == 4:
                    im = im_terms[1] - im_terms[3]
                    imag = im if imag is None else imag + im
                else:
                    im = im_terms[1] + im_terms[2]
                    if im_terms[0] < 0:
                        imag = -im if imag is None else imag - im
                    else:
                        imag = im if imag is None else imag + im
            line.append((real, imag))
        out.append(line)
    return out


def exponential(packed, scale):
    a0, a1, r01, s01, r02, s02, r12, s12 = [packed(c) * scale for c in range(8)]
    a2 = -(a0 + a1)
    h01, h02, h12 = (s01, -r01), (s02, -r02), (s12, -r12)
    n01, n02, n12 = (s01 * s01 + r01 * r01, s02 * s02 + r02 * r02, s12 * s12 + r12 * r12)
    d0, d1, d2 = a0 * a0, a1 * a1, a2 * a2
    p = 0.5 * (d0 + d1 + d2) + (n01 + n02 + n12)

    def cmul(x, y):
        return (x[0] * y[0] - x[1] * y[1], x[0] * y[1] + x[1] * y[0])

    def cmul_conj(x, y):
        return (x[0] * y[0] + x[1] * y[1], x[1] * y[0] - x[0] * y[1])

    m = cmul(h01, h12)
    q = a0 * a1 * a2 + 2.0 * (m[0] * h02[0] + m[1] * h02[1]) - a0 * n12 - a1 * n02 - a2 * n01
    k01 = cmul_conj(h02, h12)
    k12 = cmul_conj(h02, h01)
    g01 = (k01[0] - a2 * h01[0], k01[1] - a2 * h01[1])
    g02 = (m[0] - a1 * h02[0], m[1] - a1 * h02[1])
    g12 = (k12[0] - a0 * h12[0], k12[1] - a0 * h12[1])
    g00, g11, g22 = d0 + n01 + n02, d1 + n01 + n12, d2 + n02 + n12
    assert taylor_degree == 6
    c2 = -1.0 / 30.0
    f0 = (None, (c2 / 4.0) * q)
    f1 = (None, 0.25 + (c2 / 4.0) * p)
    f2r = -1.0 / 20.0
    t0 = f2r * q
    u0r, u0i = 1.0 + f2r * p, f0[1]
    w = f1[1]
    f0 = (1.0, t0 * (1.0 / 3.0))
    f1 = (-u0i * (1.0 / 3.0), u0r * (1.0 / 3.0))
    f2 = (-w * (1.0 / 3.0), None)
    t0 = f2[0] * q
    u0r, u0i = 1.0 + f2[0] * p, f0[1]
    f0 = (1.0, t0 * 0.5)
    f2 = (-f1[1] * 0.5, f1[0] * 0.5)
    f1 = (-u0i * 0.5, u0r * 0.5)
    f0, f1, f2 = (
        (1.0 - f2[1] * q, f2[0] * q),
        (-(f0[1] + f2[1] * p), 1.0 + f2[0] * p),
        (-f1[1], f1[0]),
    )

    def pair(h, g):
        rr = f1[0] * h[0] + f2[0] * g[0]
        ii = f1[1] * h[1] + f2[1] * g[1]
        ri = f1[0] * h[1] + f2[0] * g[1]
        ir = f1[1] * h[0] + f2[1] * g[0]
        return (rr - ii, ri + ir), (rr + ii, ir - ri)

    def diag(a, g):
        return (f0[0] + f1[0] * a + f2[0] * g, f0[1] + f1[1] * a + f2[1] * g)

    e01, e10 = pair(h01, g01)
    e02, e20 = pair(h02, g02)
    e12, e21 = pair(h12, g12)
    return [
        [diag(a0, g00), e01, e02],
        [e10, diag(a1, g11), e12],
        [e20, e21, diag(a2, g22)],
    ]


def store_matrix(ref, lead, matrix):
    for i in range(3):
        for j in range(3):
            for part in range(2):
                ref[lead + ((i * 3 + j) * 2 + part,)] = matrix[i][j][part]


def updated(packed, entry):
    return product(exponential(packed, time_step), load_matrix(entry))


def link_shift_y(value, amount, row, lane):
    if amount == 1:
        rolled = roll(value, -NZ, 1)
        inside = lane < 128 - NZ
    else:
        rolled = roll(value, NZ, 1)
        inside = lane >= NZ
    other = jnp.where(row % 2 == 1, roll(rolled, 1, 0), roll(rolled, -1, 0))
    return jnp.where(inside, rolled, other)


def vector_shift_y(value, amount, lane):
    if amount == 1:
        rolled = roll(value, -NZ, 1)
        inside = lane < 128 - NZ
    else:
        rolled = roll(value, NZ, 1)
        inside = lane >= NZ
    return jnp.where(inside, rolled, roll(rolled, 4, 0))


def shift_z(value, amount, lane):
    if amount == 1:
        return jnp.where(lane % NZ == NZ - 1, roll(value, NZ - 1, 1), roll(value, -1, 1))
    return jnp.where(lane % NZ == 0, roll(value, -(NZ - 1), 1), roll(value, 1, 1))


def force(own, halo, forward, work):
    row, lane = iotas()
    direction = row // 2
    is_dir = [direction == d for d in range(4)]
    for c in range(18):
        value = own(c)
        ahead = [
            halo(0, c),
            halo(2, c),
            link_shift_y(value, 1, row, lane),
            shift_z(value, 1, lane),
        ]
        for k in range(1, 4):
            forward[k - 1, c] = jnp.where(
                is_dir[0],
                ahead[k % 4],
                jnp.where(
                    is_dir[1], ahead[(1 + k) % 4], jnp.where(is_dir[2], ahead[(2 + k) % 4], ahead[(3 + k) % 4])
                ),
            )

    def turned(value, k):
        return roll(value, -2 * k, 0)

    def base(c):
        return jnp.where(is_dir[0], halo(1, c), jnp.where(is_dir[1], halo(3, c), own(c)))

    def corner_ahead(k, c):
        plain = turned(forward[3 - k, c], k)
        if k == 1:
            moved = turned(shift_z(turned(base(c), 2), 1, lane), -1)
            return jnp.where(is_dir[3], moved, jnp.where(is_dir[0], halo(0, c), plain))
        start = turned(base(c), 2)
        if k == 2:
            return jnp.where(
                is_dir[2],
                link_shift_y(start, 1, row, lane),
                jnp.where(is_dir[3], shift_z(start, 1, lane), plain),
            )
        moved = turned(link_shift_y(start, 1, row, lane), 1)
        return jnp.where(is_dir[1], halo(2, c), jnp.where(is_dir[2], moved, plain))

    def here(k, c):
        value = own(c)
        time_row, space_row = {1: (3, 0), 2: (2, 3), 3: (1, 2)}[k]
        return jnp.where(is_dir[time_row], halo(1, c), jnp.where(is_dir[space_row], halo(3, c), value))

    for k in range(1, 4):
        up = product(
            load_matrix(lambda c: turned(forward[3 - k, c], k)),
            load_matrix(lambda c: forward[k - 1, c]),
            right_h=True,
        )
        up = product(up, load_matrix(lambda c: turned(own(c), k)), right_h=True)
        low = product(load_matrix(lambda c: here(k, c)), load_matrix(lambda c: corner_ahead(k, c)))
        low = product(low, load_matrix(lambda c: turned(base(c), k)), left_h=True)
        direct = {1: is_dir[0] | is_dir[3], 2: is_dir[2] | is_dir[3], 3: is_dir[1] | is_dir[2]}[k]
        for c in range(18):
            i, j, part = c // 6, (c // 2) % 3, c % 2
            staple, down = up[i][j][part], low[i][j][part]
            staple = staple + jnp.where(direct, down, 0.0)
            if k == 1:
                work[0, c], work[1, c], work[2, c] = staple, down, down
            else:
                y_row, z_row = {2: (0, 1), 3: (3, 0)}[k]
                work[0, c] = work[0, c] + staple
                work[1, c] = jnp.where(is_dir[y_row], down, work[1, c])
                work[2, c] = jnp.where(is_dir[z_row], down, work[2, c])

    def staples(c):
        y_part = jnp.where(is_dir[2], 0.0, link_shift_y(work[1, c], -1, row, lane))
        z_part = jnp.where(is_dir[3], 0.0, shift_z(work[2, c], -1, lane))
        return work[0, c] + y_part + z_part

    total = product(load_matrix(own), load_matrix(staples))
    mean = (total[0][0][1] + total[1][1][1] + total[2][2][1]) * (1.0 / 3.0)
    factor = coupling / 3.0
    out = [(total[0][0][1] - mean) * factor, (total[1][1][1] - mean) * factor]
    for i, j in ((0, 1), (0, 2), (1, 2)):
        out.append((total[i][j][0] - total[j][i][0]) * (0.5 * factor))
        out.append((total[i][j][1] + total[j][i][1]) * (0.5 * factor))
    return out


def halo_entries(place, count, pair_ref, sides_ref, across_ref):
    row, _ = iotas()
    odd_time, odd_space = place
    first = odd_space == 0

    def corner(c):
        value = across_ref[odd_space, count + c // 2]
        return roll(value, 4, 0) if c % 2 else value

    def entry(h, c):
        if h == 0:
            value = sides_ref[odd_time, 1, odd_space, c]
            extra = jnp.where(first, corner(c), sides_ref[odd_time, 1, 1 - odd_space, c])
            return jnp.where(row < 2, roll(extra, -2, 0), value)
        if h == 1:
            return sides_ref[1 - odd_time, 0, odd_space, c]
        near, far = pair_ref[1 - odd_space, c], across_ref[odd_space, c]
        if h == 2:
            value = jnp.where(first, near, far)
            extra = jnp.where(first, sides_ref[1 - odd_time, 0, 1 - odd_space, c], corner(c))
            return jnp.where(row // 2 == 1, roll(extra, 2, 0), value)
        return jnp.where(first, far, near)

    return entry


def split_kernel(place_ref, links_ref, momenta_ref, vectors_ref, own_ref, packed_ref, fields_ref):
    half = place_ref[2]
    for c in range(18):
        for d in range(4):
            own_ref[c, 2 * d : 2 * d + 2, :] = links_ref[d * 36 + 2 * c : d * 36 + 2 * c + 2, :]
    for slot, c in enumerate(PACKED):
        for d in range(4):
            packed_ref[slot, 2 * d : 2 * d + 2, :] = momenta_ref[d * 36 + 2 * c : d * 36 + 2 * c + 2, :]
    for c in range(6):
        for block in range(2):
            tiles = []
            for h in range(2):
                parts = [
                    vectors_ref[pl.ds(block * 96 + c * 4 + h * 2 + side, 4, stride=24), :] for side in range(2)
                ]
                tiles.append(jnp.concatenate(parts, axis=0))
            fields_ref[c * 4 + block] = jnp.where(half == 0, tiles[0], tiles[1])
            fields_ref[c * 4 + 2 + block] = jnp.where(half == 0, tiles[1], tiles[0])


PACKED = (1, 9, 2, 3, 4, 5, 10, 11)


def bundle_kernel(count, extra, place_ref, own_ref, sides_ref, *rest):
    row, _ = iotas()
    odd_time, odd_space = place_ref[0], place_ref[1]
    out_ref = rest[-1]

    def corner(c):
        ahead = sides_ref[odd_time, 1, odd_space, c]
        behind = sides_ref[1 - odd_time, 0, odd_space, c]
        return jnp.where(row < 2, behind, ahead)

    for c in range(count):
        out_ref[c] = own_ref[c]
    for pair in range(count // 2):
        out_ref[count + pair] = jnp.where(row < 4, corner(2 * pair), roll(corner(2 * pair + 1), 4, 0))
    for c in range(extra):
        out_ref[count + count // 2 + c] = rest[0][c]


def first_kernel(place_ref, own_ref, packed_ref, pair_ref, sides_ref, across_ref, halo_ref, next_ref, forward, work):
    entry = halo_entries((place_ref[0], place_ref[1]), 18, pair_ref, sides_ref, across_ref)
    for h in range(4):
        for c in range(18):
            halo_ref[h, c] = entry(h, c)
    kick = force(lambda c: own_ref[c], lambda h, c: halo_ref[h, c], forward, work)
    for c in range(8):
        next_ref[c] = packed_ref[c] - (0.5 * time_step) * kick[c]


def drift(place_ref, own_ref, halo_ref, packed_ref, pair_ref, sides_ref, across_ref, new_own_ref, new_halo_ref):
    entry = halo_entries((place_ref[0], place_ref[1]), 8, pair_ref, sides_ref, across_ref)
    store_matrix(new_own_ref, (), updated(lambda c: packed_ref[c], lambda c: own_ref[c]))
    for h in range(4):
        store_matrix(new_halo_ref, (h,), updated(lambda c: entry(h, c), lambda c: halo_ref[h, c]))


def middle_kernel(
    place_ref, own_ref, halo_ref, packed_ref, pair_ref, sides_ref, across_ref,
    new_own_ref, new_halo_ref, next_ref, forward, work,
):
    drift(place_ref, own_ref, halo_ref, packed_ref, pair_ref, sides_ref, across_ref, new_own_ref, new_halo_ref)
    kick = force(lambda c: new_own_ref[c], lambda h, c: new_halo_ref[h, c], forward, work)
    for c in range(8):
        next_ref[c] = packed_ref[c] - time_step * kick[c]


def last_drift_kernel(
    place_ref, own_ref, halo_ref, packed_ref, pair_ref, sides_ref, across_ref, new_own_ref, new_halo_ref, spatial_ref
):
    drift(place_ref, own_ref, halo_ref, packed_ref, pair_ref, sides_ref, across_ref, new_own_ref, new_halo_ref)
    row, _ = iotas()
    for c in range(18):
        spatial_ref[c] = jnp.where(row < 2, roll(new_halo_ref[3, c], -2, 0), new_own_ref[c])


def last_force_kernel(own_ref, halo_ref, packed_ref, links_ref, momenta_ref, forward, work):
    kick = force(lambda c: own_ref[c], lambda h, c: halo_ref[h, c], forward, work)
    final = [packed_ref[c] - (0.5 * time_step) * kick[c] for c in range(8)]
    a0, a1, r01, s01, r02, s02, r12, s12 = final
    zero = jnp.zeros(TILE, F32)
    full = [zero, a0, r01, s01, r02, s02, -r01, s01, zero, a1, r12, s12, -r02, s02, -r12, s12, zero, -(a0 + a1)]
    for c in range(18):
        value = own_ref[c]
        for d in range(4):
            links_ref[d * 36 + 2 * c : d * 36 + 2 * c + 2, :] = value[2 * d : 2 * d + 2, :]
            momenta_ref[d * 36 + 2 * c : d * 36 + 2 * c + 2, :] = full[c][2 * d : 2 * d + 2, :]


def hopping(place_ref, spatial_ref, field_ref, near_ref, across_ref, offset, emit):
    row, lane = iotas()
    odd_space, half = place_ref[1], place_ref[2]
    first = odd_space == 0
    for side in range(2):
        owner = half if side == 0 else 1 - half

        def link(d, c):
            low = jnp.broadcast_to(spatial_ref[owner, c, 2 * d : 2 * d + 1, :], TILE)
            high = jnp.broadcast_to(spatial_ref[owner, c, 2 * d + 1 : 2 * d + 2, :], TILE)
            return jnp.where(row < 4, low, high)

        totals = {}
        for d in range(4):
            matrix = load_matrix(lambda c: link(d, c))
            for block in range(2):
                def tile(c):
                    return c * 4 + side * 2 + block

                def times(vector, dagger):
                    out = []
                    for i in range(3):
                        real, imag = None, None
                        for k in range(3):
                            ar, ai = matrix[k][i] if dagger else matrix[i][k]
                            br, bi = vector[2 * k], vector[2 * k + 1]
                            if dagger:
                                re, im = ar * br + ai * bi, ar * bi - ai * br
                            else:
                                re, im = ar * br - ai * bi, ar * bi + ai * br
                            real = re if real is None else real + re
                            imag = im if imag is None else imag + im
                        out += [real, imag]
                    return out

                if d < 2:
                    vector = []
                    for c in range(6):
                        near, far = near_ref[1 - odd_space, tile(c)], across_ref[odd_space, offset + tile(c)]
                        vector.append(jnp.where(first, near, far) if d == 1 else jnp.where(first, far, near))
                    parts = [times(vector, d == 0)]
                else:
                    values = [field_ref[tile(c)] for c in range(6)]
                    back = times(values, True)
                    if d == 2:
                        ahead = times([vector_shift_y(v, 1, lane) for v in values], False)
                        parts = [ahead, [vector_shift_y(v, -1, lane) for v in back]]
                    else:
                        ahead = times([shift_z(v, 1, lane) for v in values], False)
                        parts = [ahead, [shift_z(v, -1, lane) for v in back]]
                for part in parts:
                    for c in range(6):
                        old = totals.get((block, c))
                        totals[block, c] = part[c] if old is None else old + part[c]
        for block in range(2):
            for c in range(6):
                emit(c * 4 + side * 2 + block, totals[block, c] * (-1.0 / 6.0))


def first_hop_kernel(offset, place_ref, spatial_ref, field_ref, near_ref, across_ref, out_ref):
    def emit(tile, value):
        out_ref[tile] = value

    hopping(place_ref, spatial_ref, field_ref, near_ref, across_ref, offset, emit)


def next_hop_kernel(place_ref, spatial_ref, field_ref, older_ref, near_ref, across_ref, out_ref):
    def emit(tile, value):
        out_ref[tile] = 2.0 * value - older_ref[tile]

    hopping(place_ref, spatial_ref, field_ref, near_ref, across_ref, 0, emit)


def last_hop_kernel(
    place_ref, coefficients_ref, spatial_ref, field_ref, older_ref, oldest_ref, near_ref, across_ref, out_ref, work
):
    half = place_ref[2]

    def emit(tile, value):
        newest = 2.0 * value - older_ref[tile]
        total = coefficients_ref[0] * oldest_ref[tile] + coefficients_ref[1] * older_ref[tile]
        work[tile] = total + coefficients_ref[2] * field_ref[tile] + coefficients_ref[3] * newest

    hopping(place_ref, spatial_ref, field_ref, near_ref, across_ref, 0, emit)
    for c in range(6):
        for block in range(2):
            mine, theirs = work[c * 4 + block], work[c * 4 + 2 + block]
            for h in range(2):
                value = jnp.where(half == h, mine, theirs)
                for side in range(2):
                    out_ref[pl.ds(block * 96 + c * 4 + h * 2 + side, 4, stride=24), :] = value[4 * side : 4 * side + 4, :]


def call(kernel, shapes, inputs, scratch=(), scalars=1):
    smem = pl.BlockSpec(memory_space=pltpu.SMEM)
    vmem = pl.BlockSpec(memory_space=pltpu.VMEM)
    outs = [jax.ShapeDtypeStruct(shape, F32) for shape in shapes]
    result = pl.pallas_call(
        kernel,
        out_shape=outs,
        in_specs=[smem] * scalars + [vmem] * (len(inputs) - scalars),
        out_specs=[vmem] * len(outs),
        scratch_shapes=[pltpu.VMEM(shape + TILE, F32) for shape in scratch],
    )(*inputs)
    return result


def pairs(mesh):
    times, spaces = mesh.shape["grp"] * mesh.shape["ta"], mesh.shape["xyz"]
    offset = mesh.shape["ta"]

    def at(t, x):
        return (t % times) * spaces + x % spaces

    chip = [[at(t, x), at(t, x + 1)] for t in range(times) for x in range(0, spaces, 2)]
    across = [[at(t, x), at(t, x + 1)] for t in range(times) for x in range(1, spaces, 2)]
    time = [[at(t, x), at(t + 1, x)] for x in range(spaces) for t in range(x % 2, times, 2)]
    halves = [[at(t, x), at(t + offset, x)] for t in range(offset) for x in range(spaces)]
    return chip, across, time, halves


def body(groups, links, momenta, vectors, coefficients):
    chip, across, time, halves = groups

    def meet(values, which):
        return lax.all_gather(values, AXES, axis_index_groups=which)

    t = lax.axis_index(("grp", "ta"))
    x = lax.axis_index("xyz")
    place = jnp.stack([t % 2, x % 2, lax.axis_index("grp")]).astype(jnp.int32)
    own, packed, fields = call(
        split_kernel,
        [(18,) + TILE, (8,) + TILE, (24,) + TILE],
        [place, links.reshape(144, 128), momenta.reshape(144, 128), vectors.reshape(192, 128)],
    )
    forces = [(3, 18), (3, 18)]

    def exchange(values, extra=None):
        count = values.shape[0]
        near = meet(values, chip)
        sides = meet(meet(near, time), chip)
        inputs = [place, values, sides] + ([] if extra is None else [extra])
        more = 0 if extra is None else extra.shape[0]
        (sent,) = call(
            functools.partial(bundle_kernel, count, more), [(count + count // 2 + more,) + TILE], inputs
        )
        return near, sides, meet(sent, across)

    near, sides, far = exchange(own, fields)
    fields_near, fields_far = meet(fields, chip), far
    halo, packed = call(
        first_kernel, [(4, 18) + TILE, (8,) + TILE], [place, own, packed, near, sides, far], forces
    )
    own, halo, packed = call(
        middle_kernel,
        [(18,) + TILE, (4, 18) + TILE, (8,) + TILE],
        [place, own, halo, packed, *exchange(packed)],
        forces,
    )
    own, halo, spatial = call(
        last_drift_kernel,
        [(18,) + TILE, (4, 18) + TILE, (18,) + TILE],
        [place, own, halo, packed, *exchange(packed)],
    )
    spatial = meet(spatial, halves)
    (one,) = call(
        functools.partial(first_hop_kernel, 27),
        [(24,) + TILE],
        [place, spatial, fields, fields_near, fields_far],
    )
    (two,) = call(
        next_hop_kernel,
        [(24,) + TILE],
        [place, spatial, one, fields, meet(one, chip), meet(one, across)],
    )
    new_links, new_momenta = call(
        last_force_kernel, [(144, 128), (144, 128)], [own, halo, packed], forces, scalars=0
    )
    (filtered,) = call(
        last_hop_kernel,
        [(192, 128)],
        [place, coefficients, spatial, two, one, fields, meet(two, chip), meet(two, across)],
        [(24,)],
        scalars=2,
    )
    return (
        new_links.reshape(links.shape),
        new_momenta.reshape(momenta.shape),
        filtered.reshape(vectors.shape),
    )


def solution(mesh):
    return jax.shard_map(
        functools.partial(body, pairs(mesh)),
        mesh=mesh,
        in_specs=(
            P(None, None, None, None, ("grp", "ta"), "xyz", None),
            P(None, None, None, None, ("grp", "ta"), "xyz", None),
            P("grp", None, None, None, "ta", "xyz", None),
            P(),
        ),
        out_specs=(
            P(None, None, None, None, ("grp", "ta"), "xyz", None),
            P(None, None, None, None, ("grp", "ta"), "xyz", None),
            P("grp", None, None, None, "ta", "xyz", None),
        ),
        check_vma=False,
    )
```

```python
import functools

import jax
import jax.numpy as jnp
from jax import lax
from jax.experimental import pallas as pl
from jax.experimental.pallas import tpu as pltpu
from jax.sharding import PartitionSpec as P

NZ = 32
NSTEP = 2
NCHEB = 3
coupling = 5.7
time_step = 0.1
taylor_degree = 6

AXES = ("grp", "ta", "xyz")
TILE = (8, 128)
F32 = jnp.float32


def roll(value, shift, axis):
    return pltpu.roll(value, shift % value.shape[axis], axis)


def iotas():
    row = lax.broadcasted_iota(jnp.int32, TILE, 0)
    lane = lax.broadcasted_iota(jnp.int32, TILE, 1)
    return row, lane


def load_matrix(entry):
    return [[(entry((i * 3 + j) * 2), entry((i * 3 + j) * 2 + 1)) for j in range(3)] for i in range(3)]


def product(left, right, left_h=False, right_h=False):
    out = []
    for i in range(3):
        line = []
        for j in range(3):
            real, imag = None, None
            for k in range(3):
                ar, ai = left[k][i] if left_h else left[i][k]
                br, bi = right[j][k] if right_h else right[k][j]
                rr, ii, ri, ir = ar * br, ai * bi, ar * bi, ai * br
                re = rr + ii if left_h != right_h else rr - ii
                if left_h and right_h:
                    im_terms = (-1, ri, ir)
                elif left_h:
                    im_terms = (1, ri, -1, ir)
                elif right_h:
                    im_terms = (1, ir, -1, ri)
                else:
                    im_terms = (1, ri, ir)
                real = re if real is None else real + re
                if len(im_terms) == 4:
                    im = im_terms[1] - im_terms[3]
                    imag = im if imag is None else imag + im
                else:
                    im = im_terms[1] + im_terms[2]
                    if im_terms[0] < 0:
                        imag = -im if imag is None else imag - im
                    else:
                        imag = im if imag is None else imag + im
            line.append((real, imag))
        out.append(line)
    return out


def exponential(packed, scale):
    a0, a1, r01, s01, r02, s02, r12, s12 = [packed(c) * scale for c in range(8)]
    a2 = -(a0 + a1)
    h01, h02, h12 = (s01, -r01), (s02, -r02), (s12, -r12)
    n01, n02, n12 = (s01 * s01 + r01 * r01, s02 * s02 + r02 * r02, s12 * s12 + r12 * r12)
    d0, d1, d2 = a0 * a0, a1 * a1, a2 * a2
    p = 0.5 * (d0 + d1 + d2) + (n01 + n02 + n12)

    def cmul(x, y):
        return (x[0] * y[0] - x[1] * y[1], x[0] * y[1] + x[1] * y[0])

    def cmul_conj(x, y):
        return (x[0] * y[0] + x[1] * y[1], x[1] * y[0] - x[0] * y[1])

    m = cmul(h01, h12)
    q = a0 * a1 * a2 + 2.0 * (m[0] * h02[0] + m[1] * h02[1]) - a0 * n12 - a1 * n02 - a2 * n01
    k01 = cmul_conj(h02, h12)
    k12 = cmul_conj(h02, h01)
    g01 = (k01[0] - a2 * h01[0], k01[1] - a2 * h01[1])
    g02 = (m[0] - a1 * h02[0], m[1] - a1 * h02[1])
    g12 = (k12[0] - a0 * h12[0], k12[1] - a0 * h12[1])
    g00, g11, g22 = d0 + n01 + n02, d1 + n01 + n12, d2 + n02 + n12
    assert taylor_degree == 6
    c2 = -1.0 / 30.0
    f0 = (None, (c2 / 4.0) * q)
    f1 = (None, 0.25 + (c2 / 4.0) * p)
    f2r = -1.0 / 20.0
    t0 = f2r * q
    u0r, u0i = 1.0 + f2r * p, f0[1]
    w = f1[1]
    f0 = (1.0, t0 * (1.0 / 3.0))
    f1 = (-u0i * (1.0 / 3.0), u0r * (1.0 / 3.0))
    f2 = (-w * (1.0 / 3.0), None)
    t0 = f2[0] * q
    u0r, u0i = 1.0 + f2[0] * p, f0[1]
    f0 = (1.0, t0 * 0.5)
    f2 = (-f1[1] * 0.5, f1[0] * 0.5)
    f1 = (-u0i * 0.5, u0r * 0.5)
    f0, f1, f2 = (
        (1.0 - f2[1] * q, f2[0] * q),
        (-(f0[1] + f2[1] * p), 1.0 + f2[0] * p),
        (-f1[1], f1[0]),
    )

    def pair(h, g):
        rr = f1[0] * h[0] + f2[0] * g[0]
        ii = f1[1] * h[1] + f2[1] * g[1]
        ri = f1[0] * h[1] + f2[0] * g[1]
        ir = f1[1] * h[0] + f2[1] * g[0]
        return (rr - ii, ri + ir), (rr + ii, ir - ri)

    def diag(a, g):
        return (f0[0] + f1[0] * a + f2[0] * g, f0[1] + f1[1] * a + f2[1] * g)

    e01, e10 = pair(h01, g01)
    e02, e20 = pair(h02, g02)
    e12, e21 = pair(h12, g12)
    return [
        [diag(a0, g00), e01, e02],
        [e10, diag(a1, g11), e12],
        [e20, e21, diag(a2, g22)],
    ]


def store_matrix(ref, lead, matrix):
    for i in range(3):
        for j in range(3):
            for part in range(2):
                ref[lead + ((i * 3 + j) * 2 + part,)] = matrix[i][j][part]


def updated(packed, entry):
    return product(exponential(packed, time_step), load_matrix(entry))


def link_shift_y(value, amount, row, lane):
    if amount == 1:
        rolled = roll(value, -NZ, 1)
        inside = lane < 128 - NZ
    else:
        rolled = roll(value, NZ, 1)
        inside = lane >= NZ
    other = jnp.where(row % 2 == 1, roll(rolled, 1, 0), roll(rolled, -1, 0))
    return jnp.where(inside, rolled, other)


def vector_shift_y(value, amount, lane):
    if amount == 1:
        rolled = roll(value, -NZ, 1)
        inside = lane < 128 - NZ
    else:
        rolled = roll(value, NZ, 1)
        inside = lane >= NZ
    return jnp.where(inside, rolled, roll(rolled, 4, 0))


def shift_z(value, amount, lane):
    if amount == 1:
        return jnp.where(lane % NZ == NZ - 1, roll(value, NZ - 1, 1), roll(value, -1, 1))
    return jnp.where(lane % NZ == 0, roll(value, -(NZ - 1), 1), roll(value, 1, 1))


def force(own, halo, forward, work):
    row, lane = iotas()
    direction = row // 2
    is_dir = [direction == d for d in range(4)]
    for c in range(18):
        value = own(c)
        ahead = [
            halo(0, c),
            halo(2, c),
            link_shift_y(value, 1, row, lane),
            shift_z(value, 1, lane),
        ]
        for k in range(1, 4):
            forward[k - 1, c] = jnp.where(
                is_dir[0],
                ahead[k % 4],
                jnp.where(
                    is_dir[1], ahead[(1 + k) % 4], jnp.where(is_dir[2], ahead[(2 + k) % 4], ahead[(3 + k) % 4])
                ),
            )

    def turned(value, k):
        return roll(value, -2 * k, 0)

    def base(c):
        return jnp.where(is_dir[0], halo(1, c), jnp.where(is_dir[1], halo(3, c), own(c)))

    def corner_ahead(k, c):
        plain = turned(forward[3 - k, c], k)
        if k == 1:
            moved = turned(shift_z(turned(base(c), 2), 1, lane), -1)
            return jnp.where(is_dir[3], moved, jnp.where(is_dir[0], halo(0, c), plain))
        start = turned(base(c), 2)
        if k == 2:
            return jnp.where(
                is_dir[2],
                link_shift_y(start, 1, row, lane),
                jnp.where(is_dir[3], shift_z(start, 1, lane), plain),
            )
        moved = turned(link_shift_y(start, 1, row, lane), 1)
        return jnp.where(is_dir[1], halo(2, c), jnp.where(is_dir[2], moved, plain))

    def here(k, c):
        value = own(c)
        time_row, space_row = {1: (3, 0), 2: (2, 3), 3: (1, 2)}[k]
        return jnp.where(is_dir[time_row], halo(1, c), jnp.where(is_dir[space_row], halo(3, c), value))

    for k in range(1, 4):
        up = product(
            load_matrix(lambda c: turned(forward[3 - k, c], k)),
            load_matrix(lambda c: forward[k - 1, c]),
            right_h=True,
        )
        up = product(up, load_matrix(lambda c: turned(own(c), k)), right_h=True)
        low = product(load_matrix(lambda c: here(k, c)), load_matrix(lambda c: corner_ahead(k, c)))
        low = product(low, load_matrix(lambda c: turned(base(c), k)), left_h=True)
        direct = {1: is_dir[0] | is_dir[3], 2: is_dir[2] | is_dir[3], 3: is_dir[1] | is_dir[2]}[k]
        for c in range(18):
            i, j, part = c // 6, (c // 2) % 3, c % 2
            staple, down = up[i][j][part], low[i][j][part]
            staple = staple + jnp.where(direct, down, 0.0)
            if k == 1:
                work[0, c], work[1, c], work[2, c] = staple, down, down
            else:
                y_row, z_row = {2: (0, 1), 3: (3, 0)}[k]
                work[0, c] = work[0, c] + staple
                work[1, c] = jnp.where(is_dir[y_row], down, work[1, c])
                work[2, c] = jnp.where(is_dir[z_row], down, work[2, c])

    def staples(c):
        y_part = jnp.where(is_dir[2], 0.0, link_shift_y(work[1, c], -1, row, lane))
        z_part = jnp.where(is_dir[3], 0.0, shift_z(work[2, c], -1, lane))
        return work[0, c] + y_part + z_part

    total = product(load_matrix(own), load_matrix(staples))
    mean = (total[0][0][1] + total[1][1][1] + total[2][2][1]) * (1.0 / 3.0)
    factor = coupling / 3.0
    out = [(total[0][0][1] - mean) * factor, (total[1][1][1] - mean) * factor]
    for i, j in ((0, 1), (0, 2), (1, 2)):
        out.append((total[i][j][0] - total[j][i][0]) * (0.5 * factor))
        out.append((total[i][j][1] + total[j][i][1]) * (0.5 * factor))
    return out


def halo_entries(place, count, pair_ref, sides_ref, across_ref):
    row, _ = iotas()
    odd_time, odd_space = place
    first = odd_space == 0

    def corner(c):
        value = across_ref[odd_space, count + c // 2]
        return roll(value, 4, 0) if c % 2 else value

    def entry(h, c):
        if h == 0:
            value = sides_ref[odd_time, 1, odd_space, c]
            extra = jnp.where(first, corner(c), sides_ref[odd_time, 1, 1 - odd_space, c])
            return jnp.where(row < 2, roll(extra, -2, 0), value)
        if h == 1:
            return sides_ref[1 - odd_time, 0, odd_space, c]
        near, far = pair_ref[1 - odd_space, c], across_ref[odd_space, c]
        if h == 2:
            value = jnp.where(first, near, far)
            extra = jnp.where(first, sides_ref[1 - odd_time, 0, 1 - odd_space, c], corner(c))
            return jnp.where(row // 2 == 1, roll(extra, 2, 0), value)
        return jnp.where(first, far, near)

    return entry


def split_kernel(place_ref, links_ref, momenta_ref, vectors_ref, own_ref, packed_ref, fields_ref):
    half = place_ref[2]
    for c in range(18):
        for d in range(4):
            own_ref[c, 2 * d : 2 * d + 2, :] = links_ref[d * 36 + 2 * c : d * 36 + 2 * c + 2, :]
    for slot, c in enumerate(PACKED):
        for d in range(4):
            packed_ref[slot, 2 * d : 2 * d + 2, :] = momenta_ref[d * 36 + 2 * c : d * 36 + 2 * c + 2, :]
    for c in range(6):
        for block in range(2):
            tiles = []
            for h in range(2):
                parts = [
                    vectors_ref[pl.ds(block * 96 + c * 4 + h * 2 + side, 4, stride=24), :] for side in range(2)
                ]
                tiles.append(jnp.concatenate(parts, axis=0))
            fields_ref[c * 4 + block] = jnp.where(half == 0, tiles[0], tiles[1])
            fields_ref[c * 4 + 2 + block] = jnp.where(half == 0, tiles[1], tiles[0])


PACKED = (1, 9, 2, 3, 4, 5, 10, 11)


def bundle_kernel(count, extra, place_ref, own_ref, sides_ref, *rest):
    row, _ = iotas()
    odd_time, odd_space = place_ref[0], place_ref[1]
    out_ref = rest[-1]

    def corner(c):
        ahead = sides_ref[odd_time, 1, odd_space, c]
        behind = sides_ref[1 - odd_time, 0, odd_space, c]
        return jnp.where(row < 2, behind, ahead)

    for c in range(count):
        out_ref[c] = own_ref[c]
    for pair in range(count // 2):
        out_ref[count + pair] = jnp.where(row < 4, corner(2 * pair), roll(corner(2 * pair + 1), 4, 0))
    for c in range(extra):
        out_ref[count + count // 2 + c] = rest[0][c]


def first_kernel(place_ref, own_ref, packed_ref, pair_ref, sides_ref, across_ref, halo_ref, next_ref, forward, work):
    entry = halo_entries((place_ref[0], place_ref[1]), 18, pair_ref, sides_ref, across_ref)
    for h in range(4):
        for c in range(18):
            halo_ref[h, c] = entry(h, c)
    kick = force(lambda c: own_ref[c], lambda h, c: halo_ref[h, c], forward, work)
    for c in range(8):
        next_ref[c] = packed_ref[c] - (0.5 * time_step) * kick[c]


def drift(place_ref, own_ref, halo_ref, packed_ref, pair_ref, sides_ref, across_ref, new_own_ref, new_halo_ref):
    entry = halo_entries((place_ref[0], place_ref[1]), 8, pair_ref, sides_ref, across_ref)
    store_matrix(new_own_ref, (), updated(lambda c: packed_ref[c], lambda c: own_ref[c]))
    for h in range(4):
        store_matrix(new_halo_ref, (h,), updated(lambda c: entry(h, c), lambda c: halo_ref[h, c]))


def middle_kernel(
    place_ref, own_ref, halo_ref, packed_ref, pair_ref, sides_ref, across_ref,
    new_own_ref, new_halo_ref, next_ref, forward, work,
):
    drift(place_ref, own_ref, halo_ref, packed_ref, pair_ref, sides_ref, across_ref, new_own_ref, new_halo_ref)
    kick = force(lambda c: new_own_ref[c], lambda h, c: new_halo_ref[h, c], forward, work)
    for c in range(8):
        next_ref[c] = packed_ref[c] - time_step * kick[c]


def last_drift_kernel(
    place_ref, own_ref, halo_ref, packed_ref, pair_ref, sides_ref, across_ref, new_own_ref, new_halo_ref, spatial_ref
):
    drift(place_ref, own_ref, halo_ref, packed_ref, pair_ref, sides_ref, across_ref, new_own_ref, new_halo_ref)
    row, _ = iotas()
    for c in range(18):
        spatial_ref[c] = jnp.where(row < 2, roll(new_halo_ref[3, c], -2, 0), new_own_ref[c])


def last_force_kernel(own_ref, halo_ref, packed_ref, links_ref, momenta_ref, forward, work):
    kick = force(lambda c: own_ref[c], lambda h, c: halo_ref[h, c], forward, work)
    final = [packed_ref[c] - (0.5 * time_step) * kick[c] for c in range(8)]
    a0, a1, r01, s01, r02, s02, r12, s12 = final
    zero = jnp.zeros(TILE, F32)
    full = [zero, a0, r01, s01, r02, s02, -r01, s01, zero, a1, r12, s12, -r02, s02, -r12, s12, zero, -(a0 + a1)]
    for c in range(18):
        value = own_ref[c]
        for d in range(4):
            links_ref[d * 36 + 2 * c : d * 36 + 2 * c + 2, :] = value[2 * d : 2 * d + 2, :]
            momenta_ref[d * 36 + 2 * c : d * 36 + 2 * c + 2, :] = full[c][2 * d : 2 * d + 2, :]


def hopping(place_ref, spatial_ref, field_ref, near_ref, across_ref, offset, emit):
    row, lane = iotas()
    odd_space, half = place_ref[1], place_ref[2]
    first = odd_space == 0
    for side in range(2):
        owner = half if side == 0 else 1 - half

        def link(d, c):
            low = jnp.broadcast_to(spatial_ref[owner, c, 2 * d : 2 * d + 1, :], TILE)
            high = jnp.broadcast_to(spatial_ref[owner, c, 2 * d + 1 : 2 * d + 2, :], TILE)
            return jnp.where(row < 4, low, high)

        totals = {}
        for d in range(4):
            matrix = load_matrix(lambda c: link(d, c))
            for block in range(2):
                def tile(c):
                    return c * 4 + side * 2 + block

                def times(vector, dagger):
                    out = []
                    for i in range(3):
                        real, imag = None, None
                        for k in range(3):
                            ar, ai = matrix[k][i] if dagger else matrix[i][k]
                            br, bi = vector[2 * k], vector[2 * k + 1]
                            if dagger:
                                re, im = ar * br + ai * bi, ar * bi - ai * br
                            else:
                                re, im = ar * br - ai * bi, ar * bi + ai * br
                            real = re if real is None else real + re
                            imag = im if imag is None else imag + im
                        out += [real, imag]
                    return out

                if d < 2:
                    vector = []
                    for c in range(6):
                        near, far = near_ref[1 - odd_space, tile(c)], across_ref[odd_space, offset + tile(c)]
                        vector.append(jnp.where(first, near, far) if d == 1 else jnp.where(first, far, near))
                    parts = [times(vector, d == 0)]
                else:
                    values = [field_ref[tile(c)] for c in range(6)]
                    back = times(values, True)
                    if d == 2:
                        ahead = times([vector_shift_y(v, 1, lane) for v in values], False)
                        parts = [ahead, [vector_shift_y(v, -1, lane) for v in back]]
                    else:
                        ahead = times([shift_z(v, 1, lane) for v in values], False)
                        parts = [ahead, [shift_z(v, -1, lane) for v in back]]
                for part in parts:
                    for c in range(6):
                        old = totals.get((block, c))
                        totals[block, c] = part[c] if old is None else old + part[c]
        for block in range(2):
            for c in range(6):
                emit(c * 4 + side * 2 + block, totals[block, c] * (-1.0 / 6.0))


def first_hop_kernel(offset, place_ref, spatial_ref, field_ref, near_ref, across_ref, out_ref):
    def emit(tile, value):
        out_ref[tile] = value

    hopping(place_ref, spatial_ref, field_ref, near_ref, across_ref, offset, emit)


def next_hop_kernel(place_ref, spatial_ref, field_ref, older_ref, near_ref, across_ref, out_ref):
    def emit(tile, value):
        out_ref[tile] = 2.0 * value - older_ref[tile]

    hopping(place_ref, spatial_ref, field_ref, near_ref, across_ref, 0, emit)


def last_hop_kernel(
    place_ref, coefficients_ref, spatial_ref, field_ref, older_ref, oldest_ref, near_ref, across_ref, out_ref, work
):
    half = place_ref[2]

    def emit(tile, value):
        newest = 2.0 * value - older_ref[tile]
        total = coefficients_ref[0] * oldest_ref[tile] + coefficients_ref[1] * older_ref[tile]
        work[tile] = total + coefficients_ref[2] * field_ref[tile] + coefficients_ref[3] * newest

    hopping(place_ref, spatial_ref, field_ref, near_ref, across_ref, 0, emit)
    for c in range(6):
        for block in range(2):
            mine, theirs = work[c * 4 + block], work[c * 4 + 2 + block]
            for h in range(2):
                value = jnp.where(half == h, mine, theirs)
                for side in range(2):
                    out_ref[pl.ds(block * 96 + c * 4 + h * 2 + side, 4, stride=24), :] = value[4 * side : 4 * side + 4, :]


def call(kernel, shapes, inputs, scratch=(), scalars=1):
    smem = pl.BlockSpec(memory_space=pltpu.SMEM)
    vmem = pl.BlockSpec(memory_space=pltpu.VMEM)
    outs = [jax.ShapeDtypeStruct(shape, F32) for shape in shapes]
    result = pl.pallas_call(
        kernel,
        out_shape=outs,
        in_specs=[smem] * scalars + [vmem] * (len(inputs) - scalars),
        out_specs=[vmem] * len(outs),
        scratch_shapes=[pltpu.VMEM(shape + TILE, F32) for shape in scratch],
        compiler_params=pltpu.CompilerParams(vmem_limit_bytes=8 << 20),
    )(*inputs)
    return result


def pairs(mesh):
    times, spaces = mesh.shape["grp"] * mesh.shape["ta"], mesh.shape["xyz"]
    offset = mesh.shape["ta"]

    def at(t, x):
        return (t % times) * spaces + x % spaces

    chip = [[at(t, x), at(t, x + 1)] for t in range(times) for x in range(0, spaces, 2)]
    across = [[at(t, x), at(t, x + 1)] for t in range(times) for x in range(1, spaces, 2)]
    time = [[at(t, x), at(t + 1, x)] for x in range(spaces) for t in range(x % 2, times, 2)]
    halves = [[at(t, x), at(t + offset, x)] for t in range(offset) for x in range(spaces)]
    return chip, across, time, halves


def body(groups, links, momenta, vectors, coefficients):
    chip, across, time, halves = groups

    def meet(values, which):
        return lax.all_gather(values, AXES, axis_index_groups=which)

    t = lax.axis_index(("grp", "ta"))
    x = lax.axis_index("xyz")
    place = jnp.stack([t % 2, x % 2, lax.axis_index("grp")]).astype(jnp.int32)
    own, packed, fields = call(
        split_kernel,
        [(18,) + TILE, (8,) + TILE, (24,) + TILE],
        [place, links.reshape(144, 128), momenta.reshape(144, 128), vectors.reshape(192, 128)],
    )
    forces = [(3, 18), (3, 18)]

    def exchange(values, extra=None):
        count = values.shape[0]
        near = meet(values, chip)
        sides = meet(meet(near, time), chip)
        inputs = [place, values, sides] + ([] if extra is None else [extra])
        more = 0 if extra is None else extra.shape[0]
        (sent,) = call(
            functools.partial(bundle_kernel, count, more), [(count + count // 2 + more,) + TILE], inputs
        )
        return near, sides, meet(sent, across)

    near, sides, far = exchange(own, fields)
    fields_near, fields_far = meet(fields, chip), far
    halo, packed = call(
        first_kernel, [(4, 18) + TILE, (8,) + TILE], [place, own, packed, near, sides, far], forces
    )
    own, halo, packed = call(
        middle_kernel,
        [(18,) + TILE, (4, 18) + TILE, (8,) + TILE],
        [place, own, halo, packed, *exchange(packed)],
        forces,
    )
    own, halo, spatial = call(
        last_drift_kernel,
        [(18,) + TILE, (4, 18) + TILE, (18,) + TILE],
        [place, own, halo, packed, *exchange(packed)],
    )
    spatial = meet(spatial, halves)
    (one,) = call(
        functools.partial(first_hop_kernel, 27),
        [(24,) + TILE],
        [place, spatial, fields, fields_near, fields_far],
    )
    (two,) = call(
        next_hop_kernel,
        [(24,) + TILE],
        [place, spatial, one, fields, meet(one, chip), meet(one, across)],
    )
    new_links, new_momenta = call(
        last_force_kernel, [(144, 128), (144, 128)], [own, halo, packed], forces, scalars=0
    )
    (filtered,) = call(
        last_hop_kernel,
        [(192, 128)],
        [place, coefficients, spatial, two, one, fields, meet(two, chip), meet(two, across)],
        [(24,)],
        scalars=2,
    )
    return (
        new_links.reshape(links.shape),
        new_momenta.reshape(momenta.shape),
        filtered.reshape(vectors.shape),
    )


def solution(mesh):
    return jax.shard_map(
        functools.partial(body, pairs(mesh)),
        mesh=mesh,
        in_specs=(
            P(None, None, None, None, ("grp", "ta"), "xyz", None),
            P(None, None, None, None, ("grp", "ta"), "xyz", None),
            P("grp", None, None, None, "ta", "xyz", None),
            P(),
        ),
        out_specs=(
            P(None, None, None, None, ("grp", "ta"), "xyz", None),
            P(None, None, None, None, ("grp", "ta"), "xyz", None),
            P("grp", None, None, None, "ta", "xyz", None),
        ),
        check_vma=False,
    )
```

```python
import functools

import jax
import jax.numpy as jnp
from jax import lax
from jax.experimental import pallas as pl
from jax.experimental.pallas import tpu as pltpu
from jax.sharding import PartitionSpec as P

NZ = 32
NSTEP = 2
NCHEB = 3
coupling = 5.7
time_step = 0.1
taylor_degree = 6

AXES = ("grp", "ta", "xyz")
TILE = (8, 128)
F32 = jnp.float32


def roll(value, shift, axis):
    return pltpu.roll(value, shift % value.shape[axis], axis)


def iotas():
    row = lax.broadcasted_iota(jnp.int32, TILE, 0)
    lane = lax.broadcasted_iota(jnp.int32, TILE, 1)
    return row, lane


def load_matrix(entry):
    return [[(entry((i * 3 + j) * 2), entry((i * 3 + j) * 2 + 1)) for j in range(3)] for i in range(3)]


def product(left, right, left_h=False, right_h=False):
    out = []
    for i in range(3):
        line = []
        for j in range(3):
            real, imag = None, None
            for k in range(3):
                ar, ai = left[k][i] if left_h else left[i][k]
                br, bi = right[j][k] if right_h else right[k][j]
                rr, ii, ri, ir = ar * br, ai * bi, ar * bi, ai * br
                re = rr + ii if left_h != right_h else rr - ii
                if left_h and right_h:
                    im_terms = (-1, ri, ir)
                elif left_h:
                    im_terms = (1, ri, -1, ir)
                elif right_h:
                    im_terms = (1, ir, -1, ri)
                else:
                    im_terms = (1, ri, ir)
                real = re if real is None else real + re
                if len(im_terms) == 4:
                    im = im_terms[1] - im_terms[3]
                    imag = im if imag is None else imag + im
                else:
                    im = im_terms[1] + im_terms[2]
                    if im_terms[0] < 0:
                        imag = -im if imag is None else imag - im
                    else:
                        imag = im if imag is None else imag + im
            line.append((real, imag))
        out.append(line)
    return out


def exponential(packed, scale):
    a0, a1, r01, s01, r02, s02, r12, s12 = [packed(c) * scale for c in range(8)]
    a2 = -(a0 + a1)
    h01, h02, h12 = (s01, -r01), (s02, -r02), (s12, -r12)
    n01, n02, n12 = (s01 * s01 + r01 * r01, s02 * s02 + r02 * r02, s12 * s12 + r12 * r12)
    d0, d1, d2 = a0 * a0, a1 * a1, a2 * a2
    p = 0.5 * (d0 + d1 + d2) + (n01 + n02 + n12)

    def cmul(x, y):
        return (x[0] * y[0] - x[1] * y[1], x[0] * y[1] + x[1] * y[0])

    def cmul_conj(x, y):
        return (x[0] * y[0] + x[1] * y[1], x[1] * y[0] - x[0] * y[1])

    m = cmul(h01, h12)
    q = a0 * a1 * a2 + 2.0 * (m[0] * h02[0] + m[1] * h02[1]) - a0 * n12 - a1 * n02 - a2 * n01
    k01 = cmul_conj(h02, h12)
    k12 = cmul_conj(h02, h01)
    g01 = (k01[0] - a2 * h01[0], k01[1] - a2 * h01[1])
    g02 = (m[0] - a1 * h02[0], m[1] - a1 * h02[1])
    g12 = (k12[0] - a0 * h12[0], k12[1] - a0 * h12[1])
    g00, g11, g22 = d0 + n01 + n02, d1 + n01 + n12, d2 + n02 + n12
    assert taylor_degree == 6
    c2 = -1.0 / 30.0
    f0 = (None, (c2 / 4.0) * q)
    f1 = (None, 0.25 + (c2 / 4.0) * p)
    f2r = -1.0 / 20.0
    t0 = f2r * q
    u0r, u0i = 1.0 + f2r * p, f0[1]
    w = f1[1]
    f0 = (1.0, t0 * (1.0 / 3.0))
    f1 = (-u0i * (1.0 / 3.0), u0r * (1.0 / 3.0))
    f2 = (-w * (1.0 / 3.0), None)
    t0 = f2[0] * q
    u0r, u0i = 1.0 + f2[0] * p, f0[1]
    f0 = (1.0, t0 * 0.5)
    f2 = (-f1[1] * 0.5, f1[0] * 0.5)
    f1 = (-u0i * 0.5, u0r * 0.5)
    f0, f1, f2 = (
        (1.0 - f2[1] * q, f2[0] * q),
        (-(f0[1] + f2[1] * p), 1.0 + f2[0] * p),
        (-f1[1], f1[0]),
    )

    def pair(h, g):
        rr = f1[0] * h[0] + f2[0] * g[0]
        ii = f1[1] * h[1] + f2[1] * g[1]
        ri = f1[0] * h[1] + f2[0] * g[1]
        ir = f1[1] * h[0] + f2[1] * g[0]
        return (rr - ii, ri + ir), (rr + ii, ir - ri)

    def diag(a, g):
        return (f0[0] + f1[0] * a + f2[0] * g, f0[1] + f1[1] * a + f2[1] * g)

    e01, e10 = pair(h01, g01)
    e02, e20 = pair(h02, g02)
    e12, e21 = pair(h12, g12)
    return [
        [diag(a0, g00), e01, e02],
        [e10, diag(a1, g11), e12],
        [e20, e21, diag(a2, g22)],
    ]


def store_matrix(ref, lead, matrix):
    for i in range(3):
        for j in range(3):
            for part in range(2):
                ref[lead + ((i * 3 + j) * 2 + part,)] = matrix[i][j][part]


def updated(packed, entry):
    return product(exponential(packed, time_step), load_matrix(entry))


def link_shift_y(value, amount, row, lane):
    if amount == 1:
        rolled = roll(value, -NZ, 1)
        inside = lane < 128 - NZ
    else:
        rolled = roll(value, NZ, 1)
        inside = lane >= NZ
    other = jnp.where(row % 2 == 1, roll(rolled, 1, 0), roll(rolled, -1, 0))
    return jnp.where(inside, rolled, other)


def vector_shift_y(value, amount, lane):
    if amount == 1:
        rolled = roll(value, -NZ, 1)
        inside = lane < 128 - NZ
    else:
        rolled = roll(value, NZ, 1)
        inside = lane >= NZ
    return jnp.where(inside, rolled, roll(rolled, 4, 0))


def shift_z(value, amount, lane):
    if amount == 1:
        return jnp.where(lane % NZ == NZ - 1, roll(value, NZ - 1, 1), roll(value, -1, 1))
    return jnp.where(lane % NZ == 0, roll(value, -(NZ - 1), 1), roll(value, 1, 1))


def force(own, halo, forward, work):
    row, lane = iotas()
    direction = row // 2
    is_dir = [direction == d for d in range(4)]
    for c in range(18):
        value = own(c)
        ahead = [
            halo(0, c),
            halo(2, c),
            link_shift_y(value, 1, row, lane),
            shift_z(value, 1, lane),
        ]
        for k in range(1, 4):
            forward[k - 1, c] = jnp.where(
                is_dir[0],
                ahead[k % 4],
                jnp.where(
                    is_dir[1], ahead[(1 + k) % 4], jnp.where(is_dir[2], ahead[(2 + k) % 4], ahead[(3 + k) % 4])
                ),
            )

    def turned(value, k):
        return roll(value, -2 * k, 0)

    def base(c):
        return jnp.where(is_dir[0], halo(1, c), jnp.where(is_dir[1], halo(3, c), own(c)))

    def corner_ahead(k, c):
        plain = turned(forward[3 - k, c], k)
        if k == 1:
            moved = turned(shift_z(turned(base(c), 2), 1, lane), -1)
            return jnp.where(is_dir[3], moved, jnp.where(is_dir[0], halo(0, c), plain))
        start = turned(base(c), 2)
        if k == 2:
            return jnp.where(
                is_dir[2],
                link_shift_y(start, 1, row, lane),
                jnp.where(is_dir[3], shift_z(start, 1, lane), plain),
            )
        moved = turned(link_shift_y(start, 1, row, lane), 1)
        return jnp.where(is_dir[1], halo(2, c), jnp.where(is_dir[2], moved, plain))

    def here(k, c):
        value = own(c)
        time_row, space_row = {1: (3, 0), 2: (2, 3), 3: (1, 2)}[k]
        return jnp.where(is_dir[time_row], halo(1, c), jnp.where(is_dir[space_row], halo(3, c), value))

    for k in range(1, 4):
        up = product(
            load_matrix(lambda c: turned(forward[3 - k, c], k)),
            load_matrix(lambda c: forward[k - 1, c]),
            right_h=True,
        )
        up = product(up, load_matrix(lambda c: turned(own(c), k)), right_h=True)
        low = product(load_matrix(lambda c: here(k, c)), load_matrix(lambda c: corner_ahead(k, c)))
        low = product(low, load_matrix(lambda c: turned(base(c), k)), left_h=True)
        direct = {1: is_dir[0] | is_dir[3], 2: is_dir[2] | is_dir[3], 3: is_dir[1] | is_dir[2]}[k]
        for c in range(18):
            i, j, part = c // 6, (c // 2) % 3, c % 2
            staple, down = up[i][j][part], low[i][j][part]
            staple = staple + jnp.where(direct, down, 0.0)
            if k == 1:
                work[0, c], work[1, c], work[2, c] = staple, down, down
            else:
                y_row, z_row = {2: (0, 1), 3: (3, 0)}[k]
                work[0, c] = work[0, c] + staple
                work[1, c] = jnp.where(is_dir[y_row], down, work[1, c])
                work[2, c] = jnp.where(is_dir[z_row], down, work[2, c])

    def staples(c):
        y_part = jnp.where(is_dir[2], 0.0, link_shift_y(work[1, c], -1, row, lane))
        z_part = jnp.where(is_dir[3], 0.0, shift_z(work[2, c], -1, lane))
        return work[0, c] + y_part + z_part

    total = product(load_matrix(own), load_matrix(staples))
    mean = (total[0][0][1] + total[1][1][1] + total[2][2][1]) * (1.0 / 3.0)
    factor = coupling / 3.0
    out = [(total[0][0][1] - mean) * factor, (total[1][1][1] - mean) * factor]
    for i, j in ((0, 1), (0, 2), (1, 2)):
        out.append((total[i][j][0] - total[j][i][0]) * (0.5 * factor))
        out.append((total[i][j][1] + total[j][i][1]) * (0.5 * factor))
    return out


def completed(entry):
    tiles = [entry(c) for c in range(12)]
    a = [(tiles[2 * j], tiles[2 * j + 1]) for j in range(3)]
    b = [(tiles[6 + 2 * j], tiles[7 + 2 * j]) for j in range(3)]
    for j in range(3):
        p, q = (j + 1) % 3, (j + 2) % 3
        real = (a[p][0] * b[q][0] - a[p][1] * b[q][1]) - (a[q][0] * b[p][0] - a[q][1] * b[p][1])
        imag = (a[p][0] * b[q][1] + a[p][1] * b[q][0]) - (a[q][0] * b[p][1] + a[q][1] * b[p][0])
        tiles += [real, -imag]
    return tiles


def paired(even, odd):
    row, _ = iotas()
    return jnp.where(row < 4, even, roll(odd, 4, 0))


def unpaired(tile, c):
    return roll(tile, 4, 0) if c % 2 else tile


PACKED = (1, 9, 2, 3, 4, 5, 10, 11)


def split_kernel(place_ref, links_hbm, momenta_hbm, vectors_hbm, own_ref, packed_ref, send_ref, links_ref, momenta_ref, vectors_ref, sems):
    half = place_ref[2]
    copies = [
        pltpu.make_async_copy(source, target, sems.at[i])
        for i, (source, target) in enumerate(
            ((links_hbm, links_ref), (vectors_hbm, vectors_ref), (momenta_hbm, momenta_ref))
        )
    ]
    for copy in copies:
        copy.start()
    copies[0].wait()
    for c in range(18):
        for d in range(4):
            value = links_ref[d * 36 + 2 * c : d * 36 + 2 * c + 2, :]
            own_ref[c, 2 * d : 2 * d + 2, :] = value
            if c < 12:
                send_ref[c, 2 * d : 2 * d + 2, :] = value
    copies[1].wait()
    for c in range(6):
        for block in range(2):
            tiles = []
            for h in range(2):
                parts = [
                    vectors_ref[pl.ds(block * 96 + c * 4 + h * 2 + side, 4, stride=24), :] for side in range(2)
                ]
                tiles.append(jnp.concatenate(parts, axis=0))
            send_ref[12 + c * 4 + block] = jnp.where(half == 0, tiles[0], tiles[1])
            send_ref[12 + c * 4 + 2 + block] = jnp.where(half == 0, tiles[1], tiles[0])
    copies[2].wait()
    for slot, c in enumerate(PACKED):
        for d in range(4):
            packed_ref[slot, 2 * d : 2 * d + 2, :] = momenta_ref[d * 36 + 2 * c : d * 36 + 2 * c + 2, :]


def first_bundle_kernel(place_ref, send_ref, packed_ref, near_ref, sides_ref, out_ref):
    row, _ = iotas()
    odd_time, odd_space = place_ref[0], place_ref[1]
    first = odd_space == 0
    for c in range(12):
        ahead = sides_ref[odd_time, 1, odd_space, c]
        ahead_other = sides_ref[odd_time, 1, 1 - odd_space, c]
        behind_other = sides_ref[1 - odd_time, 0, 1 - odd_space, c]
        partner = near_ref[1 - odd_space, c]
        out_ref[c] = send_ref[c]
        out_ref[12 + c] = jnp.where(row < 2, roll(ahead_other, -2, 0), ahead)
        out_ref[24 + c] = sides_ref[1 - odd_time, 0, odd_space, c]
        out_ref[36 + c] = jnp.where(first & (row // 2 == 1), roll(behind_other, 2, 0), partner)
    for c in range(8):
        out_ref[48 + c] = packed_ref[c]
    for c in range(24):
        out_ref[56 + c] = send_ref[12 + c]
        out_ref[80 + c] = near_ref[1 - odd_space, 12 + c]


def first_kernel(
    place_ref, own_ref, packed_ref, near_ref, sides_ref, across_ref,
    halo_ref, send_ref, far_packed_ref, forward, work, far_own, far_halo,
):
    row, _ = iotas()
    odd_time, odd_space = place_ref[0], place_ref[1]
    first = odd_space == 0
    x_row = row // 2 == 1

    def ahead(c):
        return sides_ref[odd_time, 1, odd_space, c]

    def behind(c):
        return sides_ref[1 - odd_time, 0, odd_space, c]

    def ahead_other(c):
        return sides_ref[odd_time, 1, 1 - odd_space, c]

    def behind_other(c):
        return sides_ref[1 - odd_time, 0, 1 - odd_space, c]

    def near(c):
        return near_ref[1 - odd_space, c]

    def far(group, c):
        return across_ref[odd_space, group * 12 + c]

    def own(c):
        return own_ref[c]

    def put(ref, lead, entry):
        for c, tile in enumerate(completed(entry)):
            ref[lead + (c,)] = tile

    put(halo_ref, (0,), lambda c: jnp.where(row < 2, roll(jnp.where(first, far(1, c), ahead_other(c)), -2, 0), ahead(c)))
    put(halo_ref, (1,), behind)
    put(
        halo_ref,
        (2,),
        lambda c: jnp.where(
            x_row,
            roll(jnp.where(first, behind_other(c), far(2, c)), 2, 0),
            jnp.where(first, near(c), far(0, c)),
        ),
    )
    put(halo_ref, (3,), lambda c: jnp.where(first, far(0, c), near(c)))
    put(far_own, (), lambda c: far(0, c))
    put(far_halo, (0,), lambda c: jnp.where((row < 2) & (odd_space == 1), roll(ahead(c), -2, 0), far(1, c)))
    put(far_halo, (1,), lambda c: far(2, c))
    put(far_halo, (2,), lambda c: jnp.where(first, jnp.where(x_row, roll(behind(c), 2, 0), own(c)), far(3, c)))
    put(far_halo, (3,), lambda c: jnp.where(first, far(3, c), own(c)))
    kick = force(lambda c: far_own[c], lambda h, c: far_halo[h, c], forward, work)
    moved = [far(4, c) - (0.5 * time_step) * kick[c] for c in range(8)]
    for c in range(8):
        far_packed_ref[c] = moved[c]
    for pair in range(4):
        send_ref[8 + pair] = paired(moved[2 * pair], moved[2 * pair + 1])
    kick = force(own, lambda h, c: halo_ref[h, c], forward, work)
    for c in range(8):
        send_ref[c] = packed_ref[c] - (0.5 * time_step) * kick[c]


def drift(own_ref, halo_ref, packed, entry, new_own_ref, new_halo_ref):
    store_matrix(new_own_ref, (), updated(packed, lambda c: own_ref[c]))
    for h in range(4):
        store_matrix(new_halo_ref, (h,), updated(lambda c: entry(h, c), lambda c: halo_ref[h, c]))


def middle_kernel(
    place_ref, own_ref, halo_ref, send_ref, far_packed_ref, near_ref, sides_ref,
    new_own_ref, new_halo_ref, next_ref, forward, work,
):
    row, _ = iotas()
    odd_time, odd_space = place_ref[0], place_ref[1]
    first = odd_space == 0

    def entry(h, c):
        if h == 0:
            main, corner = sides_ref[odd_time, 1, 0, c], unpaired(sides_ref[odd_time, 1, 0, 8 + c // 2], c)
            extra = jnp.where(first, corner, main)
            return jnp.where(row < 2, roll(extra, -2, 0), sides_ref[odd_time, 1, odd_space, c])
        if h == 1:
            return sides_ref[1 - odd_time, 0, odd_space, c]
        near, far = near_ref[1 - odd_space, c], far_packed_ref[c]
        if h == 2:
            main, corner = sides_ref[1 - odd_time, 0, 1, c], unpaired(sides_ref[1 - odd_time, 0, 1, 8 + c // 2], c)
            extra = jnp.where(first, main, corner)
            return jnp.where(row // 2 == 1, roll(extra, 2, 0), jnp.where(first, near, far))
        return jnp.where(first, far, near)

    drift(own_ref, halo_ref, lambda c: send_ref[c], entry, new_own_ref, new_halo_ref)
    kick = force(lambda c: new_own_ref[c], lambda h, c: new_halo_ref[h, c], forward, work)
    for c in range(8):
        next_ref[c] = send_ref[c] - time_step * kick[c]


def last_bundle_kernel(place_ref, own_ref, halo_ref, packed_ref, near_ref, sides_ref, out_ref):
    row, _ = iotas()
    odd_time, odd_space = place_ref[0], place_ref[1]
    first = odd_space == 0

    def corner(c):
        return jnp.where(row < 2, sides_ref[1 - odd_time, 0, odd_space, c], sides_ref[odd_time, 1, odd_space, c])

    for c in range(8):
        out_ref[c] = packed_ref[c]
    for pair in range(4):
        out_ref[8 + pair] = paired(corner(2 * pair), corner(2 * pair + 1))
    even = updated(
        lambda c: jnp.where(first, packed_ref[c], near_ref[1 - odd_space, c]),
        lambda c: jnp.where(first, own_ref[c], halo_ref[3, c]),
    )
    for pair in range(9):
        i, j = pair // 3, pair % 3
        out_ref[12 + pair] = paired(even[i][j][0], even[i][j][1])


def last_drift_kernel(
    place_ref, own_ref, halo_ref, packed_ref, near_ref, sides_ref, across_ref,
    new_own_ref, new_halo_ref, spatial_ref,
):
    row, _ = iotas()
    odd_time, odd_space = place_ref[0], place_ref[1]
    first = odd_space == 0
    x_row = row // 2 == 1

    def entry(h, c):
        if h == 0:
            corner = unpaired(across_ref[odd_space, 8 + c // 2], c)
            extra = jnp.where(first, corner, sides_ref[odd_time, 1, 1 - odd_space, c])
            return jnp.where(row < 2, roll(extra, -2, 0), sides_ref[odd_time, 1, odd_space, c])
        if h == 1:
            return sides_ref[1 - odd_time, 0, odd_space, c]
        near, far = near_ref[1 - odd_space, c], across_ref[odd_space, c]
        if h == 2:
            corner = unpaired(across_ref[odd_space, 8 + c // 2], c)
            extra = jnp.where(first, sides_ref[1 - odd_time, 0, 1 - odd_space, c], corner)
            return jnp.where(x_row, roll(extra, 2, 0), jnp.where(first, near, far))
        return jnp.where(first, far, near)

    drift(own_ref, halo_ref, lambda c: packed_ref[c], entry, new_own_ref, new_halo_ref)
    for c in range(18):
        own, right, left = new_own_ref[c], new_halo_ref[2, c], new_halo_ref[3, c]
        even = unpaired(across_ref[odd_space, 12 + c // 2], c)
        spatial_ref[0, c] = jnp.where(row < 2, roll(left, -2, 0), own)
        spatial_ref[1, c] = jnp.where(
            first,
            jnp.where(row < 2, roll(even, -2, 0), left),
            jnp.where(row < 2, roll(own, -2, 0), jnp.where(x_row, even, right)),
        )


def last_force_kernel(own_ref, halo_ref, packed_ref, links_ref, momenta_ref, forward, work):
    kick = force(lambda c: own_ref[c], lambda h, c: halo_ref[h, c], forward, work)
    final = [packed_ref[c] - (0.5 * time_step) * kick[c] for c in range(8)]
    a0, a1, r01, s01, r02, s02, r12, s12 = final
    zero = jnp.zeros(TILE, F32)
    full = [zero, a0, r01, s01, r02, s02, -r01, s01, zero, a1, r12, s12, -r02, s02, -r12, s12, zero, -(a0 + a1)]
    for c in range(18):
        value = own_ref[c]
        for d in range(4):
            links_ref[d * 36 + 2 * c : d * 36 + 2 * c + 2, :] = value[2 * d : 2 * d + 2, :]
            momenta_ref[d * 36 + 2 * c : d * 36 + 2 * c + 2, :] = full[c][2 * d : 2 * d + 2, :]


def hopping(half, links, field, ahead, behind, emit):
    row, lane = iotas()
    for side in range(2):
        owner = half if side == 0 else 1 - half

        def link(d, c):
            low = jnp.broadcast_to(links(owner, c, slice(2 * d, 2 * d + 1)), TILE)
            high = jnp.broadcast_to(links(owner, c, slice(2 * d + 1, 2 * d + 2)), TILE)
            return jnp.where(row < 4, low, high)

        totals = {}
        for d in range(4):
            matrix = load_matrix(lambda c: link(d, c))
            for block in range(2):

                def times(vector, dagger):
                    out = []
                    for i in range(3):
                        real, imag = None, None
                        for k in range(3):
                            ar, ai = matrix[k][i] if dagger else matrix[i][k]
                            br, bi = vector[2 * k], vector[2 * k + 1]
                            if dagger:
                                re, im = ar * br + ai * bi, ar * bi - ai * br
                            else:
                                re, im = ar * br - ai * bi, ar * bi + ai * br
                            real = re if real is None else real + re
                            imag = im if imag is None else imag + im
                        out += [real, imag]
                    return out

                tiles = [c * 4 + side * 2 + block for c in range(6)]
                if d == 0:
                    parts = [times([behind(tile) for tile in tiles], True)]
                elif d == 1:
                    parts = [times([ahead(tile) for tile in tiles], False)]
                else:
                    values = [field(tile) for tile in tiles]
                    back = times(values, True)
                    if d == 2:
                        front = times([vector_shift_y(v, 1, lane) for v in values], False)
                        parts = [front, [vector_shift_y(v, -1, lane) for v in back]]
                    else:
                        front = times([shift_z(v, 1, lane) for v in values], False)
                        parts = [front, [shift_z(v, -1, lane) for v in back]]
                for part in parts:
                    for c in range(6):
                        old = totals.get((block, c))
                        totals[block, c] = part[c] if old is None else old + part[c]
        for block in range(2):
            for c in range(6):
                emit(c * 4 + side * 2 + block, totals[block, c] * (-1.0 / 6.0))


def first_hop_kernel(place_ref, spatial_ref, field_ref, near_ref, across_ref, out_ref, far_out_ref):
    odd_space, half = place_ref[1], place_ref[2]
    first = odd_space == 0

    def own(tile):
        return field_ref[12 + tile]

    def near(tile):
        return near_ref[1 - odd_space, 12 + tile]

    def far(tile):
        return across_ref[odd_space, 56 + tile]

    def farther(tile):
        return across_ref[odd_space, 80 + tile]

    def put(ref):
        def emit(tile, value):
            ref[tile] = value

        return emit

    hopping(
        half,
        lambda owner, c, rows: spatial_ref[owner, 0, c, rows, :],
        own,
        lambda tile: jnp.where(first, near(tile), far(tile)),
        lambda tile: jnp.where(first, far(tile), near(tile)),
        put(out_ref),
    )
    hopping(
        half,
        lambda owner, c, rows: spatial_ref[owner, 1, c, rows, :],
        far,
        lambda tile: jnp.where(first, own(tile), farther(tile)),
        lambda tile: jnp.where(first, farther(tile), own(tile)),
        put(far_out_ref),
    )


def second_hop_kernel(place_ref, spatial_ref, field_ref, older_ref, near_ref, far_ref, out_ref):
    odd_space, half = place_ref[1], place_ref[2]
    first = odd_space == 0

    def near(tile):
        return near_ref[1 - odd_space, tile]

    def emit(tile, value):
        out_ref[tile] = 2.0 * value - older_ref[12 + tile]

    hopping(
        half,
        lambda owner, c, rows: spatial_ref[owner, 0, c, rows, :],
        lambda tile: field_ref[tile],
        lambda tile: jnp.where(first, near(tile), far_ref[tile]),
        lambda tile: jnp.where(first, far_ref[tile], near(tile)),
        emit,
    )


def last_hop_kernel(
    place_ref, coefficients_ref, spatial_ref, field_ref, older_ref, oldest_ref, near_ref, across_ref, out_ref, work
):
    odd_space, half = place_ref[1], place_ref[2]
    first = odd_space == 0

    def near(tile):
        return near_ref[1 - odd_space, tile]

    def far(tile):
        return across_ref[odd_space, tile]

    def emit(tile, value):
        newest = 2.0 * value - older_ref[tile]
        total = coefficients_ref[0] * oldest_ref[12 + tile] + coefficients_ref[1] * older_ref[tile]
        work[tile] = total + coefficients_ref[2] * field_ref[tile] + coefficients_ref[3] * newest

    hopping(
        half,
        lambda owner, c, rows: spatial_ref[owner, 0, c, rows, :],
        lambda tile: field_ref[tile],
        lambda tile: jnp.where(first, near(tile), far(tile)),
        lambda tile: jnp.where(first, far(tile), near(tile)),
        emit,
    )
    for c in range(6):
        for block in range(2):
            mine, theirs = work[c * 4 + block], work[c * 4 + 2 + block]
            for h in range(2):
                value = jnp.where(half == h, mine, theirs)
                for side in range(2):
                    out_ref[pl.ds(block * 96 + c * 4 + h * 2 + side, 4, stride=24), :] = value[4 * side : 4 * side + 4, :]


def call(kernel, shapes, inputs, scratch=(), scalars=1, space=pltpu.VMEM):
    smem = pl.BlockSpec(memory_space=pltpu.SMEM)
    vmem = pl.BlockSpec(memory_space=pltpu.VMEM)
    outs = [jax.ShapeDtypeStruct(shape, F32) for shape in shapes]
    return pl.pallas_call(
        kernel,
        out_shape=outs,
        in_specs=[smem] * scalars + [pl.BlockSpec(memory_space=space)] * (len(inputs) - scalars),
        out_specs=[vmem] * len(outs),
        scratch_shapes=[pltpu.VMEM(shape, F32) if isinstance(shape, tuple) else shape for shape in scratch],
        compiler_params=pltpu.CompilerParams(vmem_limit_bytes=8 << 20),
    )(*inputs)


def pairs(mesh):
    times, spaces = mesh.shape["grp"] * mesh.shape["ta"], mesh.shape["xyz"]
    offset = mesh.shape["ta"]

    def at(t, x):
        return (t % times) * spaces + x % spaces

    chip = [[at(t, x), at(t, x + 1)] for t in range(times) for x in range(0, spaces, 2)]
    across = [[at(t, x), at(t, x + 1)] for t in range(times) for x in range(1, spaces, 2)]
    time = [[at(t, x), at(t + 1, x)] for x in range(spaces) for t in range(x % 2, times, 2)]
    halves = [[at(t, x), at(t + offset, x)] for t in range(offset) for x in range(spaces)]
    return chip, across, time, halves


def body(groups, links, momenta, vectors, coefficients):
    chip, across, time, halves = groups

    def meet(values, which):
        return lax.all_gather(values, AXES, axis_index_groups=which)

    t = lax.axis_index(("grp", "ta"))
    x = lax.axis_index("xyz")
    place = jnp.stack([t % 2, x % 2, lax.axis_index("grp")]).astype(jnp.int32)
    raw = [links.reshape(144, 128), momenta.reshape(144, 128), vectors.reshape(192, 128)]
    own, packed, send = call(
        split_kernel,
        [(18,) + TILE, (8,) + TILE, (36,) + TILE],
        [place] + raw,
        [value.shape for value in raw] + [pltpu.SemaphoreType.DMA((3,))],
        space=pltpu.HBM,
    )
    forces = [(3, 18) + TILE, (3, 18) + TILE]

    near = meet(send, chip)
    sides = meet(meet(near[:, :12], time), chip)
    (bundle,) = call(first_bundle_kernel, [(104,) + TILE], [place, send, packed, near, sides])
    far = meet(bundle, across)
    halo, pushed, far_packed = call(
        first_kernel,
        [(4, 18) + TILE, (12,) + TILE, (8,) + TILE],
        [place, own, packed, near, sides, far],
        forces + [(18,) + TILE, (4, 18) + TILE],
    )
    fields, fields_near, fields_far = send, near, far

    near = meet(pushed, chip)
    sides = meet(meet(near, time), chip)
    own, halo, packed = call(
        middle_kernel,
        [(18,) + TILE, (4, 18) + TILE, (8,) + TILE],
        [place, own, halo, pushed, far_packed, near, sides],
        forces,
    )

    near = meet(packed, chip)
    sides = meet(meet(near, time), chip)
    (bundle,) = call(last_bundle_kernel, [(21,) + TILE], [place, own, halo, packed, near, sides])
    own, halo, spatial = call(
        last_drift_kernel,
        [(18,) + TILE, (4, 18) + TILE, (2, 18) + TILE],
        [place, own, halo, packed, near, sides, meet(bundle, across)],
    )

    spatial = meet(spatial, halves)
    one, far_one = call(
        first_hop_kernel, [(24,) + TILE, (24,) + TILE], [place, spatial, fields, fields_near, fields_far]
    )
    (two,) = call(second_hop_kernel, [(24,) + TILE], [place, spatial, one, fields, meet(one, chip), far_one])
    new_links, new_momenta = call(
        last_force_kernel, [(144, 128), (144, 128)], [own, halo, packed], forces, scalars=0
    )
    (filtered,) = call(
        last_hop_kernel,
        [(192, 128)],
        [place, coefficients, spatial, two, one, fields, meet(two, chip), meet(two, across)],
        [(24,) + TILE],
        scalars=2,
    )
    return (
        new_links.reshape(links.shape),
        new_momenta.reshape(momenta.shape),
        filtered.reshape(vectors.shape),
    )


def solution(mesh):
    return jax.shard_map(
        functools.partial(body, pairs(mesh)),
        mesh=mesh,
        in_specs=(
            P(None, None, None, None, ("grp", "ta"), "xyz", None),
            P(None, None, None, None, ("grp", "ta"), "xyz", None),
            P("grp", None, None, None, "ta", "xyz", None),
            P(),
        ),
        out_specs=(
            P(None, None, None, None, ("grp", "ta"), "xyz", None),
            P(None, None, None, None, ("grp", "ta"), "xyz", None),
            P("grp", None, None, None, "ta", "xyz", None),
        ),
        check_vma=False,
    )
```

```python
import functools

import jax
import jax.numpy as jnp
from jax import lax
from jax.experimental import pallas as pl
from jax.experimental.pallas import tpu as pltpu
from jax.sharding import PartitionSpec as P

NZ = 32
NSTEP = 2
NCHEB = 3
coupling = 5.7
time_step = 0.1
taylor_degree = 6

AXES = ("grp", "ta", "xyz")
TILE = (8, 128)
F32 = jnp.float32


def roll(value, shift, axis):
    return pltpu.roll(value, shift % value.shape[axis], axis)


def iotas():
    row = lax.broadcasted_iota(jnp.int32, TILE, 0)
    lane = lax.broadcasted_iota(jnp.int32, TILE, 1)
    return row, lane


def load_matrix(entry):
    return [[(entry((i * 3 + j) * 2), entry((i * 3 + j) * 2 + 1)) for j in range(3)] for i in range(3)]


def product(left, right, left_h=False, right_h=False):
    out = []
    for i in range(3):
        line = []
        for j in range(3):
            real, imag = None, None
            for k in range(3):
                ar, ai = left[k][i] if left_h else left[i][k]
                br, bi = right[j][k] if right_h else right[k][j]
                rr, ii, ri, ir = ar * br, ai * bi, ar * bi, ai * br
                re = rr + ii if left_h != right_h else rr - ii
                if left_h and right_h:
                    im_terms = (-1, ri, ir)
                elif left_h:
                    im_terms = (1, ri, -1, ir)
                elif right_h:
                    im_terms = (1, ir, -1, ri)
                else:
                    im_terms = (1, ri, ir)
                real = re if real is None else real + re
                if len(im_terms) == 4:
                    im = im_terms[1] - im_terms[3]
                    imag = im if imag is None else imag + im
                else:
                    im = im_terms[1] + im_terms[2]
                    if im_terms[0] < 0:
                        imag = -im if imag is None else imag - im
                    else:
                        imag = im if imag is None else imag + im
            line.append((real, imag))
        out.append(line)
    return out


def exponential(packed, scale):
    a0, a1, r01, s01, r02, s02, r12, s12 = [packed(c) * scale for c in range(8)]
    a2 = -(a0 + a1)
    h01, h02, h12 = (s01, -r01), (s02, -r02), (s12, -r12)
    n01, n02, n12 = (s01 * s01 + r01 * r01, s02 * s02 + r02 * r02, s12 * s12 + r12 * r12)
    d0, d1, d2 = a0 * a0, a1 * a1, a2 * a2
    p = 0.5 * (d0 + d1 + d2) + (n01 + n02 + n12)

    def cmul(x, y):
        return (x[0] * y[0] - x[1] * y[1], x[0] * y[1] + x[1] * y[0])

    def cmul_conj(x, y):
        return (x[0] * y[0] + x[1] * y[1], x[1] * y[0] - x[0] * y[1])

    m = cmul(h01, h12)
    q = a0 * a1 * a2 + 2.0 * (m[0] * h02[0] + m[1] * h02[1]) - a0 * n12 - a1 * n02 - a2 * n01
    k01 = cmul_conj(h02, h12)
    k12 = cmul_conj(h02, h01)
    g01 = (k01[0] - a2 * h01[0], k01[1] - a2 * h01[1])
    g02 = (m[0] - a1 * h02[0], m[1] - a1 * h02[1])
    g12 = (k12[0] - a0 * h12[0], k12[1] - a0 * h12[1])
    g00, g11, g22 = d0 + n01 + n02, d1 + n01 + n12, d2 + n02 + n12
    assert taylor_degree == 6
    c2 = -1.0 / 30.0
    f0 = (None, (c2 / 4.0) * q)
    f1 = (None, 0.25 + (c2 / 4.0) * p)
    f2r = -1.0 / 20.0
    t0 = f2r * q
    u0r, u0i = 1.0 + f2r * p, f0[1]
    w = f1[1]
    f0 = (1.0, t0 * (1.0 / 3.0))
    f1 = (-u0i * (1.0 / 3.0), u0r * (1.0 / 3.0))
    f2 = (-w * (1.0 / 3.0), None)
    t0 = f2[0] * q
    u0r, u0i = 1.0 + f2[0] * p, f0[1]
    f0 = (1.0, t0 * 0.5)
    f2 = (-f1[1] * 0.5, f1[0] * 0.5)
    f1 = (-u0i * 0.5, u0r * 0.5)
    f0, f1, f2 = (
        (1.0 - f2[1] * q, f2[0] * q),
        (-(f0[1] + f2[1] * p), 1.0 + f2[0] * p),
        (-f1[1], f1[0]),
    )

    def pair(h, g):
        rr = f1[0] * h[0] + f2[0] * g[0]
        ii = f1[1] * h[1] + f2[1] * g[1]
        ri = f1[0] * h[1] + f2[0] * g[1]
        ir = f1[1] * h[0] + f2[1] * g[0]
        return (rr - ii, ri + ir), (rr + ii, ir - ri)

    def diag(a, g):
        return (f0[0] + f1[0] * a + f2[0] * g, f0[1] + f1[1] * a + f2[1] * g)

    e01, e10 = pair(h01, g01)
    e02, e20 = pair(h02, g02)
    e12, e21 = pair(h12, g12)
    return [
        [diag(a0, g00), e01, e02],
        [e10, diag(a1, g11), e12],
        [e20, e21, diag(a2, g22)],
    ]


def store_matrix(ref, lead, matrix):
    for i in range(3):
        for j in range(3):
            for part in range(2):
                ref[lead + ((i * 3 + j) * 2 + part,)] = matrix[i][j][part]


def updated(packed, entry):
    return product(exponential(packed, time_step), load_matrix(entry))


def link_shift_y(value, amount, row, lane):
    if amount == 1:
        rolled = roll(value, -NZ, 1)
        inside = lane < 128 - NZ
    else:
        rolled = roll(value, NZ, 1)
        inside = lane >= NZ
    other = jnp.where(row % 2 == 1, roll(rolled, 1, 0), roll(rolled, -1, 0))
    return jnp.where(inside, rolled, other)


def vector_shift_y(value, amount, lane):
    if amount == 1:
        rolled = roll(value, -NZ, 1)
        inside = lane < 128 - NZ
    else:
        rolled = roll(value, NZ, 1)
        inside = lane >= NZ
    return jnp.where(inside, rolled, roll(rolled, 4, 0))


def shift_z(value, amount, lane):
    if amount == 1:
        return jnp.where(lane % NZ == NZ - 1, roll(value, NZ - 1, 1), roll(value, -1, 1))
    return jnp.where(lane % NZ == 0, roll(value, -(NZ - 1), 1), roll(value, 1, 1))


def force(own, halo, forward, work):
    row, lane = iotas()
    direction = row // 2
    is_dir = [direction == d for d in range(4)]
    for c in range(18):
        value = own(c)
        ahead = [
            halo(0, c),
            halo(2, c),
            link_shift_y(value, 1, row, lane),
            shift_z(value, 1, lane),
        ]
        for k in range(1, 4):
            forward[k - 1, c] = jnp.where(
                is_dir[0],
                ahead[k % 4],
                jnp.where(
                    is_dir[1], ahead[(1 + k) % 4], jnp.where(is_dir[2], ahead[(2 + k) % 4], ahead[(3 + k) % 4])
                ),
            )

    def turned(value, k):
        return roll(value, -2 * k, 0)

    def base(c):
        return jnp.where(is_dir[0], halo(1, c), jnp.where(is_dir[1], halo(3, c), own(c)))

    def corner_ahead(k, c):
        plain = turned(forward[3 - k, c], k)
        if k == 1:
            moved = turned(shift_z(turned(base(c), 2), 1, lane), -1)
            return jnp.where(is_dir[3], moved, jnp.where(is_dir[0], halo(0, c), plain))
        start = turned(base(c), 2)
        if k == 2:
            return jnp.where(
                is_dir[2],
                link_shift_y(start, 1, row, lane),
                jnp.where(is_dir[3], shift_z(start, 1, lane), plain),
            )
        moved = turned(link_shift_y(start, 1, row, lane), 1)
        return jnp.where(is_dir[1], halo(2, c), jnp.where(is_dir[2], moved, plain))

    def here(k, c):
        value = own(c)
        time_row, space_row = {1: (3, 0), 2: (2, 3), 3: (1, 2)}[k]
        return jnp.where(is_dir[time_row], halo(1, c), jnp.where(is_dir[space_row], halo(3, c), value))

    for k in range(1, 4):
        up = product(
            load_matrix(lambda c: turned(forward[3 - k, c], k)),
            load_matrix(lambda c: forward[k - 1, c]),
            right_h=True,
        )
        up = product(up, load_matrix(lambda c: turned(own(c), k)), right_h=True)
        low = product(load_matrix(lambda c: here(k, c)), load_matrix(lambda c: corner_ahead(k, c)))
        low = product(low, load_matrix(lambda c: turned(base(c), k)), left_h=True)
        direct = {1: is_dir[0] | is_dir[3], 2: is_dir[2] | is_dir[3], 3: is_dir[1] | is_dir[2]}[k]
        for c in range(18):
            i, j, part = c // 6, (c // 2) % 3, c % 2
            staple, down = up[i][j][part], low[i][j][part]
            staple = staple + jnp.where(direct, down, 0.0)
            if k == 1:
                work[0, c], work[1, c], work[2, c] = staple, down, down
            else:
                y_row, z_row = {2: (0, 1), 3: (3, 0)}[k]
                work[0, c] = work[0, c] + staple
                work[1, c] = jnp.where(is_dir[y_row], down, work[1, c])
                work[2, c] = jnp.where(is_dir[z_row], down, work[2, c])

    def staples(c):
        y_part = jnp.where(is_dir[2], 0.0, link_shift_y(work[1, c], -1, row, lane))
        z_part = jnp.where(is_dir[3], 0.0, shift_z(work[2, c], -1, lane))
        return work[0, c] + y_part + z_part

    total = product(load_matrix(own), load_matrix(staples))
    mean = (total[0][0][1] + total[1][1][1] + total[2][2][1]) * (1.0 / 3.0)
    factor = coupling / 3.0
    out = [(total[0][0][1] - mean) * factor, (total[1][1][1] - mean) * factor]
    for i, j in ((0, 1), (0, 2), (1, 2)):
        out.append((total[i][j][0] - total[j][i][0]) * (0.5 * factor))
        out.append((total[i][j][1] + total[j][i][1]) * (0.5 * factor))
    return out


def completed(entry):
    tiles = [entry(c) for c in range(12)]
    a = [(tiles[2 * j], tiles[2 * j + 1]) for j in range(3)]
    b = [(tiles[6 + 2 * j], tiles[7 + 2 * j]) for j in range(3)]
    for j in range(3):
        p, q = (j + 1) % 3, (j + 2) % 3
        real = (a[p][0] * b[q][0] - a[p][1] * b[q][1]) - (a[q][0] * b[p][0] - a[q][1] * b[p][1])
        imag = (a[p][0] * b[q][1] + a[p][1] * b[q][0]) - (a[q][0] * b[p][1] + a[q][1] * b[p][0])
        tiles += [real, -imag]
    return tiles


def paired(even, odd):
    row, _ = iotas()
    return jnp.where(row < 4, even, roll(odd, 4, 0))


def unpaired(tile, c):
    return roll(tile, 4, 0) if c % 2 else tile


PACKED = (1, 9, 2, 3, 4, 5, 10, 11)


def split_kernel(place_ref, links_hbm, momenta_hbm, vectors_hbm, own_ref, packed_ref, send_ref, links_ref, momenta_ref, vectors_ref, sems):
    half = place_ref[2]
    copies = [
        pltpu.make_async_copy(source, target, sems.at[i])
        for i, (source, target) in enumerate(
            ((links_hbm, links_ref), (vectors_hbm, vectors_ref), (momenta_hbm, momenta_ref))
        )
    ]
    for copy in copies:
        copy.start()
    copies[0].wait()
    for c in range(18):
        for d in range(4):
            value = links_ref[d * 36 + 2 * c : d * 36 + 2 * c + 2, :]
            own_ref[c, 2 * d : 2 * d + 2, :] = value
            if c < 12:
                send_ref[c, 2 * d : 2 * d + 2, :] = value
    copies[1].wait()
    for c in range(6):
        for block in range(2):
            tiles = []
            for h in range(2):
                parts = [
                    vectors_ref[pl.ds(block * 96 + c * 4 + h * 2 + side, 4, stride=24), :] for side in range(2)
                ]
                tiles.append(jnp.concatenate(parts, axis=0))
            send_ref[12 + c * 4 + block] = jnp.where(half == 0, tiles[0], tiles[1])
            send_ref[12 + c * 4 + 2 + block] = jnp.where(half == 0, tiles[1], tiles[0])
    copies[2].wait()
    for slot, c in enumerate(PACKED):
        for d in range(4):
            packed_ref[slot, 2 * d : 2 * d + 2, :] = momenta_ref[d * 36 + 2 * c : d * 36 + 2 * c + 2, :]


def first_bundle_kernel(place_ref, send_ref, packed_ref, near_ref, sides_ref, out_ref):
    row, _ = iotas()
    odd_time, odd_space = place_ref[0], place_ref[1]
    first = odd_space == 0
    for c in range(12):
        ahead = sides_ref[odd_time, 1, odd_space, c]
        ahead_other = sides_ref[odd_time, 1, 1 - odd_space, c]
        behind_other = sides_ref[1 - odd_time, 0, 1 - odd_space, c]
        partner = near_ref[1 - odd_space, c]
        out_ref[c] = send_ref[c]
        out_ref[12 + c] = jnp.where(row < 2, roll(ahead_other, -2, 0), ahead)
        out_ref[24 + c] = sides_ref[1 - odd_time, 0, odd_space, c]
        out_ref[36 + c] = jnp.where(first & (row // 2 == 1), roll(behind_other, 2, 0), partner)
    for c in range(8):
        out_ref[48 + c] = packed_ref[c]
    for c in range(24):
        out_ref[56 + c] = send_ref[12 + c]
        out_ref[80 + c] = near_ref[1 - odd_space, 12 + c]


def first_kernel(
    place_ref, own_ref, packed_ref, near_ref, sides_ref, across_ref,
    halo_ref, send_ref, far_packed_ref, forward, work, far_own, far_halo,
):
    row, _ = iotas()
    odd_time, odd_space = place_ref[0], place_ref[1]
    first = odd_space == 0
    x_row = row // 2 == 1

    def ahead(c):
        return sides_ref[odd_time, 1, odd_space, c]

    def behind(c):
        return sides_ref[1 - odd_time, 0, odd_space, c]

    def ahead_other(c):
        return sides_ref[odd_time, 1, 1 - odd_space, c]

    def behind_other(c):
        return sides_ref[1 - odd_time, 0, 1 - odd_space, c]

    def near(c):
        return near_ref[1 - odd_space, c]

    def far(group, c):
        return across_ref[odd_space, group * 12 + c]

    def own(c):
        return own_ref[c]

    def put(ref, lead, entry):
        for c, tile in enumerate(completed(entry)):
            ref[lead + (c,)] = tile

    put(halo_ref, (0,), lambda c: jnp.where(row < 2, roll(jnp.where(first, far(1, c), ahead_other(c)), -2, 0), ahead(c)))
    put(halo_ref, (1,), behind)
    put(
        halo_ref,
        (2,),
        lambda c: jnp.where(
            x_row,
            roll(jnp.where(first, behind_other(c), far(2, c)), 2, 0),
            jnp.where(first, near(c), far(0, c)),
        ),
    )
    put(halo_ref, (3,), lambda c: jnp.where(first, far(0, c), near(c)))
    put(far_own, (), lambda c: far(0, c))
    put(far_halo, (0,), lambda c: jnp.where((row < 2) & (odd_space == 1), roll(ahead(c), -2, 0), far(1, c)))
    put(far_halo, (1,), lambda c: far(2, c))
    put(far_halo, (2,), lambda c: jnp.where(first, jnp.where(x_row, roll(behind(c), 2, 0), own(c)), far(3, c)))
    put(far_halo, (3,), lambda c: jnp.where(first, far(3, c), own(c)))
    kick = force(lambda c: far_own[c], lambda h, c: far_halo[h, c], forward, work)
    moved = [far(4, c) - (0.5 * time_step) * kick[c] for c in range(8)]
    for c in range(8):
        far_packed_ref[c] = moved[c]
    for pair in range(4):
        send_ref[8 + pair] = paired(moved[2 * pair], moved[2 * pair + 1])
    kick = force(own, lambda h, c: halo_ref[h, c], forward, work)
    for c in range(8):
        send_ref[c] = packed_ref[c] - (0.5 * time_step) * kick[c]


def drift(own_ref, halo_ref, packed, entry, new_own_ref, new_halo_ref):
    store_matrix(new_own_ref, (), updated(packed, lambda c: own_ref[c]))
    for h in range(4):
        store_matrix(new_halo_ref, (h,), updated(lambda c: entry(h, c), lambda c: halo_ref[h, c]))


def middle_kernel(
    place_ref, own_ref, halo_ref, send_ref, far_packed_ref, near_ref, sides_ref,
    new_own_ref, new_halo_ref, next_ref, forward, work,
):
    row, _ = iotas()
    odd_time, odd_space = place_ref[0], place_ref[1]
    first = odd_space == 0

    def entry(h, c):
        if h == 0:
            main, corner = sides_ref[odd_time, 1, 0, c], unpaired(sides_ref[odd_time, 1, 0, 8 + c // 2], c)
            extra = jnp.where(first, corner, main)
            return jnp.where(row < 2, roll(extra, -2, 0), sides_ref[odd_time, 1, odd_space, c])
        if h == 1:
            return sides_ref[1 - odd_time, 0, odd_space, c]
        near, far = near_ref[1 - odd_space, c], far_packed_ref[c]
        if h == 2:
            main, corner = sides_ref[1 - odd_time, 0, 1, c], unpaired(sides_ref[1 - odd_time, 0, 1, 8 + c // 2], c)
            extra = jnp.where(first, main, corner)
            return jnp.where(row // 2 == 1, roll(extra, 2, 0), jnp.where(first, near, far))
        return jnp.where(first, far, near)

    drift(own_ref, halo_ref, lambda c: send_ref[c], entry, new_own_ref, new_halo_ref)
    kick = force(lambda c: new_own_ref[c], lambda h, c: new_halo_ref[h, c], forward, work)
    for c in range(8):
        next_ref[c] = send_ref[c] - time_step * kick[c]


def last_bundle_kernel(place_ref, own_ref, halo_ref, packed_ref, near_ref, sides_ref, out_ref):
    row, _ = iotas()
    odd_time, odd_space = place_ref[0], place_ref[1]
    first = odd_space == 0

    def corner(c):
        return jnp.where(row < 2, sides_ref[1 - odd_time, 0, odd_space, c], sides_ref[odd_time, 1, odd_space, c])

    for c in range(8):
        out_ref[c] = packed_ref[c]
    for pair in range(4):
        out_ref[8 + pair] = paired(corner(2 * pair), corner(2 * pair + 1))
    even = updated(
        lambda c: jnp.where(first, packed_ref[c], near_ref[1 - odd_space, c]),
        lambda c: jnp.where(first, own_ref[c], halo_ref[3, c]),
    )
    for pair in range(9):
        i, j = pair // 3, pair % 3
        out_ref[12 + pair] = paired(even[i][j][0], even[i][j][1])


def last_drift_kernel(
    place_ref, own_ref, halo_ref, packed_ref, near_ref, sides_ref, across_ref,
    new_own_ref, new_halo_ref, spatial_ref,
):
    row, _ = iotas()
    odd_time, odd_space = place_ref[0], place_ref[1]
    first = odd_space == 0
    x_row = row // 2 == 1

    def entry(h, c):
        if h == 0:
            corner = unpaired(across_ref[odd_space, 8 + c // 2], c)
            extra = jnp.where(first, corner, sides_ref[odd_time, 1, 1 - odd_space, c])
            return jnp.where(row < 2, roll(extra, -2, 0), sides_ref[odd_time, 1, odd_space, c])
        if h == 1:
            return sides_ref[1 - odd_time, 0, odd_space, c]
        near, far = near_ref[1 - odd_space, c], across_ref[odd_space, c]
        if h == 2:
            corner = unpaired(across_ref[odd_space, 8 + c // 2], c)
            extra = jnp.where(first, sides_ref[1 - odd_time, 0, 1 - odd_space, c], corner)
            return jnp.where(x_row, roll(extra, 2, 0), jnp.where(first, near, far))
        return jnp.where(first, far, near)

    drift(own_ref, halo_ref, lambda c: packed_ref[c], entry, new_own_ref, new_halo_ref)
    for c in range(18):
        own, right, left = new_own_ref[c], new_halo_ref[2, c], new_halo_ref[3, c]
        even = unpaired(across_ref[odd_space, 12 + c // 2], c)
        spatial_ref[0, c] = jnp.where(row < 2, roll(left, -2, 0), own)
        spatial_ref[1, c] = jnp.where(
            first,
            jnp.where(row < 2, roll(even, -2, 0), left),
            jnp.where(row < 2, roll(own, -2, 0), jnp.where(x_row, even, right)),
        )


def last_force_kernel(own_ref, halo_ref, packed_ref, links_ref, momenta_ref, forward, work):
    kick = force(lambda c: own_ref[c], lambda h, c: halo_ref[h, c], forward, work)
    final = [packed_ref[c] - (0.5 * time_step) * kick[c] for c in range(8)]
    a0, a1, r01, s01, r02, s02, r12, s12 = final
    zero = jnp.zeros(TILE, F32)
    full = [zero, a0, r01, s01, r02, s02, -r01, s01, zero, a1, r12, s12, -r02, s02, -r12, s12, zero, -(a0 + a1)]
    for c in range(18):
        value = own_ref[c]
        for d in range(4):
            links_ref[d * 36 + 2 * c : d * 36 + 2 * c + 2, :] = value[2 * d : 2 * d + 2, :]
            momenta_ref[d * 36 + 2 * c : d * 36 + 2 * c + 2, :] = full[c][2 * d : 2 * d + 2, :]


def hopping(half, links, field, ahead, behind, emit):
    row, lane = iotas()
    for side in range(2):
        owner = half if side == 0 else 1 - half

        def link(d, c):
            low = jnp.broadcast_to(links(owner, c, slice(2 * d, 2 * d + 1)), TILE)
            high = jnp.broadcast_to(links(owner, c, slice(2 * d + 1, 2 * d + 2)), TILE)
            return jnp.where(row < 4, low, high)

        totals = {}
        for d in range(4):
            matrix = load_matrix(lambda c: link(d, c))
            for block in range(2):

                def times(vector, dagger):
                    out = []
                    for i in range(3):
                        real, imag = None, None
                        for k in range(3):
                            ar, ai = matrix[k][i] if dagger else matrix[i][k]
                            br, bi = vector[2 * k], vector[2 * k + 1]
                            if dagger:
                                re, im = ar * br + ai * bi, ar * bi - ai * br
                            else:
                                re, im = ar * br - ai * bi, ar * bi + ai * br
                            real = re if real is None else real + re
                            imag = im if imag is None else imag + im
                        out += [real, imag]
                    return out

                tiles = [c * 4 + side * 2 + block for c in range(6)]
                if d == 0:
                    parts = [times([behind(tile) for tile in tiles], True)]
                elif d == 1:
                    parts = [times([ahead(tile) for tile in tiles], False)]
                else:
                    values = [field(tile) for tile in tiles]
                    back = times(values, True)
                    if d == 2:
                        front = times([vector_shift_y(v, 1, lane) for v in values], False)
                        parts = [front, [vector_shift_y(v, -1, lane) for v in back]]
                    else:
                        front = times([shift_z(v, 1, lane) for v in values], False)
                        parts = [front, [shift_z(v, -1, lane) for v in back]]
                for part in parts:
                    for c in range(6):
                        old = totals.get((block, c))
                        totals[block, c] = part[c] if old is None else old + part[c]
        for block in range(2):
            for c in range(6):
                emit(c * 4 + side * 2 + block, totals[block, c] * (-1.0 / 6.0))


def first_hop_kernel(place_ref, spatial_ref, field_ref, near_ref, across_ref, out_ref, far_out_ref):
    odd_space, half = place_ref[1], place_ref[2]
    first = odd_space == 0

    def own(tile):
        return field_ref[12 + tile]

    def near(tile):
        return near_ref[1 - odd_space, 12 + tile]

    def far(tile):
        return across_ref[odd_space, 56 + tile]

    def farther(tile):
        return across_ref[odd_space, 80 + tile]

    def put(ref):
        def emit(tile, value):
            ref[tile] = value

        return emit

    hopping(
        half,
        lambda owner, c, rows: spatial_ref[owner, 0, c, rows, :],
        own,
        lambda tile: jnp.where(first, near(tile), far(tile)),
        lambda tile: jnp.where(first, far(tile), near(tile)),
        put(out_ref),
    )
    hopping(
        half,
        lambda owner, c, rows: spatial_ref[owner, 1, c, rows, :],
        far,
        lambda tile: jnp.where(first, own(tile), farther(tile)),
        lambda tile: jnp.where(first, farther(tile), own(tile)),
        put(far_out_ref),
    )


def second_hop_kernel(place_ref, spatial_ref, field_ref, older_ref, near_ref, far_ref, out_ref):
    odd_space, half = place_ref[1], place_ref[2]
    first = odd_space == 0

    def near(tile):
        return near_ref[1 - odd_space, tile]

    def emit(tile, value):
        out_ref[tile] = 2.0 * value - older_ref[12 + tile]

    hopping(
        half,
        lambda owner, c, rows: spatial_ref[owner, 0, c, rows, :],
        lambda tile: field_ref[tile],
        lambda tile: jnp.where(first, near(tile), far_ref[tile]),
        lambda tile: jnp.where(first, far_ref[tile], near(tile)),
        emit,
    )


def last_hop_kernel(
    place_ref, coefficients_hbm, spatial_ref, field_ref, older_ref, oldest_ref, near_ref, across_ref,
    out_ref, work, coefficients_ref, sem,
):
    copy = pltpu.make_async_copy(coefficients_hbm, coefficients_ref, sem)
    copy.start()
    odd_space, half = place_ref[1], place_ref[2]
    first = odd_space == 0

    def near(tile):
        return near_ref[1 - odd_space, tile]

    def far(tile):
        return across_ref[odd_space, tile]

    def emit(tile, value):
        work[tile] = 2.0 * value - older_ref[tile]

    hopping(
        half,
        lambda owner, c, rows: spatial_ref[owner, 0, c, rows, :],
        lambda tile: field_ref[tile],
        lambda tile: jnp.where(first, near(tile), far(tile)),
        lambda tile: jnp.where(first, far(tile), near(tile)),
        emit,
    )
    copy.wait()

    def total(tile):
        value = coefficients_ref[0] * oldest_ref[12 + tile] + coefficients_ref[1] * older_ref[tile]
        return value + coefficients_ref[2] * field_ref[tile] + coefficients_ref[3] * work[tile]

    for c in range(6):
        for block in range(2):
            mine, theirs = total(c * 4 + block), total(c * 4 + 2 + block)
            for h in range(2):
                value = jnp.where(half == h, mine, theirs)
                for side in range(2):
                    out_ref[pl.ds(block * 96 + c * 4 + h * 2 + side, 4, stride=24), :] = value[4 * side : 4 * side + 4, :]


def call(kernel, shapes, inputs, scratch=(), scalars=1, hbm=()):
    def spec(position):
        if position < scalars:
            return pl.BlockSpec(memory_space=pltpu.SMEM)
        return pl.BlockSpec(memory_space=pltpu.HBM if position in hbm else pltpu.VMEM)

    inputs = [
        pltpu.with_memory_space_constraint(value, pltpu.HBM) if position in hbm else value
        for position, value in enumerate(inputs)
    ]
    return pl.pallas_call(
        kernel,
        out_shape=[jax.ShapeDtypeStruct(shape, F32) for shape in shapes],
        in_specs=[spec(position) for position in range(len(inputs))],
        out_specs=[pl.BlockSpec(memory_space=pltpu.VMEM)] * len(shapes),
        scratch_shapes=[pltpu.VMEM(shape, F32) if isinstance(shape, tuple) else shape for shape in scratch],
        compiler_params=pltpu.CompilerParams(vmem_limit_bytes=8 << 20),
    )(*inputs)


def pairs(mesh):
    times, spaces = mesh.shape["grp"] * mesh.shape["ta"], mesh.shape["xyz"]
    offset = mesh.shape["ta"]

    def at(t, x):
        return (t % times) * spaces + x % spaces

    chip = [[at(t, x), at(t, x + 1)] for t in range(times) for x in range(0, spaces, 2)]
    across = [[at(t, x), at(t, x + 1)] for t in range(times) for x in range(1, spaces, 2)]
    time = [[at(t, x), at(t + 1, x)] for x in range(spaces) for t in range(x % 2, times, 2)]
    halves = [[at(t, x), at(t + offset, x)] for t in range(offset) for x in range(spaces)]
    return chip, across, time, halves


def body(groups, links, momenta, vectors, coefficients):
    chip, across, time, halves = groups

    def meet(values, which):
        return lax.all_gather(values, AXES, axis_index_groups=which)

    t = lax.axis_index(("grp", "ta"))
    x = lax.axis_index("xyz")
    place = jnp.stack([t % 2, x % 2, lax.axis_index("grp")]).astype(jnp.int32)
    raw = [links.reshape(144, 128), momenta.reshape(144, 128), vectors.reshape(192, 128)]
    own, packed, send = call(
        split_kernel,
        [(18,) + TILE, (8,) + TILE, (36,) + TILE],
        [place] + raw,
        [value.shape for value in raw] + [pltpu.SemaphoreType.DMA((3,))],
        hbm=(1, 2, 3),
    )
    forces = [(3, 18) + TILE, (3, 18) + TILE]

    near = meet(send, chip)
    sides = meet(meet(near[:, :12], time), chip)
    (bundle,) = call(first_bundle_kernel, [(104,) + TILE], [place, send, packed, near, sides])
    far = meet(bundle, across)
    halo, pushed, far_packed = call(
        first_kernel,
        [(4, 18) + TILE, (12,) + TILE, (8,) + TILE],
        [place, own, packed, near, sides, far],
        forces + [(18,) + TILE, (4, 18) + TILE],
    )
    fields, fields_near, fields_far = send, near, far

    near = meet(pushed, chip)
    sides = meet(meet(near, time), chip)
    own, halo, packed = call(
        middle_kernel,
        [(18,) + TILE, (4, 18) + TILE, (8,) + TILE],
        [place, own, halo, pushed, far_packed, near, sides],
        forces,
    )

    near = meet(packed, chip)
    sides = meet(meet(near, time), chip)
    (bundle,) = call(last_bundle_kernel, [(21,) + TILE], [place, own, halo, packed, near, sides])
    own, halo, spatial = call(
        last_drift_kernel,
        [(18,) + TILE, (4, 18) + TILE, (2, 18) + TILE],
        [place, own, halo, packed, near, sides, meet(bundle, across)],
    )

    spatial = meet(spatial, halves)
    one, far_one = call(
        first_hop_kernel, [(24,) + TILE, (24,) + TILE], [place, spatial, fields, fields_near, fields_far]
    )
    (two,) = call(second_hop_kernel, [(24,) + TILE], [place, spatial, one, fields, meet(one, chip), far_one])
    new_links, new_momenta = call(
        last_force_kernel, [(144, 128), (144, 128)], [own, halo, packed], forces, scalars=0
    )
    (filtered,) = call(
        last_hop_kernel,
        [(192, 128)],
        [place, coefficients, spatial, two, one, fields, meet(two, chip), meet(two, across)],
        [(24,) + TILE, pltpu.SMEM((4,), F32), pltpu.SemaphoreType.DMA],
        hbm=(1,),
    )
    return (
        new_links.reshape(links.shape),
        new_momenta.reshape(momenta.shape),
        filtered.reshape(vectors.shape),
    )


def solution(mesh):
    return jax.shard_map(
        functools.partial(body, pairs(mesh)),
        mesh=mesh,
        in_specs=(
            P(None, None, None, None, ("grp", "ta"), "xyz", None),
            P(None, None, None, None, ("grp", "ta"), "xyz", None),
            P("grp", None, None, None, "ta", "xyz", None),
            P(),
        ),
        out_specs=(
            P(None, None, None, None, ("grp", "ta"), "xyz", None),
            P(None, None, None, None, ("grp", "ta"), "xyz", None),
            P("grp", None, None, None, "ta", "xyz", None),
        ),
        check_vma=False,
    )
```

```python
import functools

import jax
import jax.numpy as jnp
from jax import lax
from jax.experimental import pallas as pl
from jax.experimental.pallas import tpu as pltpu
from jax.sharding import PartitionSpec as P

NZ = 32
NSTEP = 2
NCHEB = 3
coupling = 5.7
time_step = 0.1
taylor_degree = 6

AXES = ("grp", "ta", "xyz")
TILE = (8, 128)
F32 = jnp.float32


def roll(value, shift, axis):
    return pltpu.roll(value, shift % value.shape[axis], axis)


def iotas():
    row = lax.broadcasted_iota(jnp.int32, TILE, 0)
    lane = lax.broadcasted_iota(jnp.int32, TILE, 1)
    return row, lane


def load_matrix(entry):
    return [[(entry((i * 3 + j) * 2), entry((i * 3 + j) * 2 + 1)) for j in range(3)] for i in range(3)]


def product(left, right, left_h=False, right_h=False):
    out = []
    for i in range(3):
        line = []
        for j in range(3):
            real, imag = None, None
            for k in range(3):
                ar, ai = left[k][i] if left_h else left[i][k]
                br, bi = right[j][k] if right_h else right[k][j]
                rr, ii, ri, ir = ar * br, ai * bi, ar * bi, ai * br
                re = rr + ii if left_h != right_h else rr - ii
                if left_h and right_h:
                    im_terms = (-1, ri, ir)
                elif left_h:
                    im_terms = (1, ri, -1, ir)
                elif right_h:
                    im_terms = (1, ir, -1, ri)
                else:
                    im_terms = (1, ri, ir)
                real = re if real is None else real + re
                if len(im_terms) == 4:
                    im = im_terms[1] - im_terms[3]
                    imag = im if imag is None else imag + im
                else:
                    im = im_terms[1] + im_terms[2]
                    if im_terms[0] < 0:
                        imag = -im if imag is None else imag - im
                    else:
                        imag = im if imag is None else imag + im
            line.append((real, imag))
        out.append(line)
    return out


def exponential(packed, scale):
    a0, a1, r01, s01, r02, s02, r12, s12 = [packed(c) * scale for c in range(8)]
    a2 = -(a0 + a1)
    h01, h02, h12 = (s01, -r01), (s02, -r02), (s12, -r12)
    n01, n02, n12 = (s01 * s01 + r01 * r01, s02 * s02 + r02 * r02, s12 * s12 + r12 * r12)
    d0, d1, d2 = a0 * a0, a1 * a1, a2 * a2
    p = 0.5 * (d0 + d1 + d2) + (n01 + n02 + n12)

    def cmul(x, y):
        return (x[0] * y[0] - x[1] * y[1], x[0] * y[1] + x[1] * y[0])

    def cmul_conj(x, y):
        return (x[0] * y[0] + x[1] * y[1], x[1] * y[0] - x[0] * y[1])

    m = cmul(h01, h12)
    q = a0 * a1 * a2 + 2.0 * (m[0] * h02[0] + m[1] * h02[1]) - a0 * n12 - a1 * n02 - a2 * n01
    k01 = cmul_conj(h02, h12)
    k12 = cmul_conj(h02, h01)
    g01 = (k01[0] - a2 * h01[0], k01[1] - a2 * h01[1])
    g02 = (m[0] - a1 * h02[0], m[1] - a1 * h02[1])
    g12 = (k12[0] - a0 * h12[0], k12[1] - a0 * h12[1])
    g00, g11, g22 = d0 + n01 + n02, d1 + n01 + n12, d2 + n02 + n12
    assert taylor_degree == 6
    c2 = -1.0 / 30.0
    f0 = (None, (c2 / 4.0) * q)
    f1 = (None, 0.25 + (c2 / 4.0) * p)
    f2r = -1.0 / 20.0
    t0 = f2r * q
    u0r, u0i = 1.0 + f2r * p, f0[1]
    w = f1[1]
    f0 = (1.0, t0 * (1.0 / 3.0))
    f1 = (-u0i * (1.0 / 3.0), u0r * (1.0 / 3.0))
    f2 = (-w * (1.0 / 3.0), None)
    t0 = f2[0] * q
    u0r, u0i = 1.0 + f2[0] * p, f0[1]
    f0 = (1.0, t0 * 0.5)
    f2 = (-f1[1] * 0.5, f1[0] * 0.5)
    f1 = (-u0i * 0.5, u0r * 0.5)
    f0, f1, f2 = (
        (1.0 - f2[1] * q, f2[0] * q),
        (-(f0[1] + f2[1] * p), 1.0 + f2[0] * p),
        (-f1[1], f1[0]),
    )

    def pair(h, g):
        rr = f1[0] * h[0] + f2[0] * g[0]
        ii = f1[1] * h[1] + f2[1] * g[1]
        ri = f1[0] * h[1] + f2[0] * g[1]
        ir = f1[1] * h[0] + f2[1] * g[0]
        return (rr - ii, ri + ir), (rr + ii, ir - ri)

    def diag(a, g):
        return (f0[0] + f1[0] * a + f2[0] * g, f0[1] + f1[1] * a + f2[1] * g)

    e01, e10 = pair(h01, g01)
    e02, e20 = pair(h02, g02)
    e12, e21 = pair(h12, g12)
    return [
        [diag(a0, g00), e01, e02],
        [e10, diag(a1, g11), e12],
        [e20, e21, diag(a2, g22)],
    ]


def store_matrix(ref, lead, matrix):
    for i in range(3):
        for j in range(3):
            for part in range(2):
                ref[lead + ((i * 3 + j) * 2 + part,)] = matrix[i][j][part]


def updated(packed, entry):
    return product(exponential(packed, time_step), load_matrix(entry))


def link_shift_y(value, amount, row, lane):
    if amount == 1:
        rolled = roll(value, -NZ, 1)
        inside = lane < 128 - NZ
    else:
        rolled = roll(value, NZ, 1)
        inside = lane >= NZ
    other = jnp.where(row % 2 == 1, roll(rolled, 1, 0), roll(rolled, -1, 0))
    return jnp.where(inside, rolled, other)


def vector_shift_y(value, amount, lane):
    if amount == 1:
        rolled = roll(value, -NZ, 1)
        inside = lane < 128 - NZ
    else:
        rolled = roll(value, NZ, 1)
        inside = lane >= NZ
    return jnp.where(inside, rolled, roll(rolled, 4, 0))


def shift_z(value, amount, lane):
    if amount == 1:
        return jnp.where(lane % NZ == NZ - 1, roll(value, NZ - 1, 1), roll(value, -1, 1))
    return jnp.where(lane % NZ == 0, roll(value, -(NZ - 1), 1), roll(value, 1, 1))


def force(own, halo, forward, work):
    row, lane = iotas()
    direction = row // 2
    is_dir = [direction == d for d in range(4)]
    for c in range(18):
        value = own(c)
        ahead = [
            halo(0, c),
            halo(2, c),
            link_shift_y(value, 1, row, lane),
            shift_z(value, 1, lane),
        ]
        for k in range(1, 4):
            forward[k - 1, c] = jnp.where(
                is_dir[0],
                ahead[k % 4],
                jnp.where(
                    is_dir[1], ahead[(1 + k) % 4], jnp.where(is_dir[2], ahead[(2 + k) % 4], ahead[(3 + k) % 4])
                ),
            )

    def turned(value, k):
        return roll(value, -2 * k, 0)

    def base(c):
        return jnp.where(is_dir[0], halo(1, c), jnp.where(is_dir[1], halo(3, c), own(c)))

    def corner_ahead(k, c):
        plain = turned(forward[3 - k, c], k)
        if k == 1:
            moved = turned(shift_z(turned(base(c), 2), 1, lane), -1)
            return jnp.where(is_dir[3], moved, jnp.where(is_dir[0], halo(0, c), plain))
        start = turned(base(c), 2)
        if k == 2:
            return jnp.where(
                is_dir[2],
                link_shift_y(start, 1, row, lane),
                jnp.where(is_dir[3], shift_z(start, 1, lane), plain),
            )
        moved = turned(link_shift_y(start, 1, row, lane), 1)
        return jnp.where(is_dir[1], halo(2, c), jnp.where(is_dir[2], moved, plain))

    def here(k, c):
        value = own(c)
        time_row, space_row = {1: (3, 0), 2: (2, 3), 3: (1, 2)}[k]
        return jnp.where(is_dir[time_row], halo(1, c), jnp.where(is_dir[space_row], halo(3, c), value))

    for k in range(1, 4):
        up = product(
            load_matrix(lambda c: turned(forward[3 - k, c], k)),
            load_matrix(lambda c: forward[k - 1, c]),
            right_h=True,
        )
        up = product(up, load_matrix(lambda c: turned(own(c), k)), right_h=True)
        low = product(load_matrix(lambda c: here(k, c)), load_matrix(lambda c: corner_ahead(k, c)))
        low = product(low, load_matrix(lambda c: turned(base(c), k)), left_h=True)
        direct = {1: is_dir[0] | is_dir[3], 2: is_dir[2] | is_dir[3], 3: is_dir[1] | is_dir[2]}[k]
        for c in range(18):
            i, j, part = c // 6, (c // 2) % 3, c % 2
            staple, down = up[i][j][part], low[i][j][part]
            staple = staple + jnp.where(direct, down, 0.0)
            if k == 1:
                work[0, c], work[1, c], work[2, c] = staple, down, down
            else:
                y_row, z_row = {2: (0, 1), 3: (3, 0)}[k]
                work[0, c] = work[0, c] + staple
                work[1, c] = jnp.where(is_dir[y_row], down, work[1, c])
                work[2, c] = jnp.where(is_dir[z_row], down, work[2, c])

    def staples(c):
        y_part = jnp.where(is_dir[2], 0.0, link_shift_y(work[1, c], -1, row, lane))
        z_part = jnp.where(is_dir[3], 0.0, shift_z(work[2, c], -1, lane))
        return work[0, c] + y_part + z_part

    total = product(load_matrix(own), load_matrix(staples))
    mean = (total[0][0][1] + total[1][1][1] + total[2][2][1]) * (1.0 / 3.0)
    factor = coupling / 3.0
    out = [(total[0][0][1] - mean) * factor, (total[1][1][1] - mean) * factor]
    for i, j in ((0, 1), (0, 2), (1, 2)):
        out.append((total[i][j][0] - total[j][i][0]) * (0.5 * factor))
        out.append((total[i][j][1] + total[j][i][1]) * (0.5 * factor))
    return out


def completed(entry):
    tiles = [entry(c) for c in range(12)]
    a = [(tiles[2 * j], tiles[2 * j + 1]) for j in range(3)]
    b = [(tiles[6 + 2 * j], tiles[7 + 2 * j]) for j in range(3)]
    for j in range(3):
        p, q = (j + 1) % 3, (j + 2) % 3
        real = (a[p][0] * b[q][0] - a[p][1] * b[q][1]) - (a[q][0] * b[p][0] - a[q][1] * b[p][1])
        imag = (a[p][0] * b[q][1] + a[p][1] * b[q][0]) - (a[q][0] * b[p][1] + a[q][1] * b[p][0])
        tiles += [real, -imag]
    return tiles


def paired(even, odd):
    row, _ = iotas()
    return jnp.where(row < 4, even, roll(odd, 4, 0))


def unpaired(tile, c):
    return roll(tile, 4, 0) if c % 2 else tile


PACKED = (1, 9, 2, 3, 4, 5, 10, 11)


def split_kernel(place_ref, links_hbm, momenta_hbm, vectors_hbm, own_ref, packed_ref, send_ref, links_ref, momenta_ref, vectors_ref, sems):
    half = place_ref[2]
    copies = [
        pltpu.make_async_copy(source, target, sems.at[i])
        for i, (source, target) in enumerate(
            ((links_hbm, links_ref), (vectors_hbm, vectors_ref), (momenta_hbm, momenta_ref))
        )
    ]
    for copy in copies:
        copy.start()
    copies[0].wait()
    for c in range(18):
        for d in range(4):
            value = links_ref[d * 36 + 2 * c : d * 36 + 2 * c + 2, :]
            own_ref[c, 2 * d : 2 * d + 2, :] = value
            if c < 12:
                send_ref[c, 2 * d : 2 * d + 2, :] = value
    copies[1].wait()
    for c in range(6):
        for block in range(2):
            tiles = []
            for h in range(2):
                parts = [
                    vectors_ref[pl.ds(block * 96 + c * 4 + h * 2 + side, 4, stride=24), :] for side in range(2)
                ]
                tiles.append(jnp.concatenate(parts, axis=0))
            send_ref[12 + c * 4 + block] = jnp.where(half == 0, tiles[0], tiles[1])
            send_ref[12 + c * 4 + 2 + block] = jnp.where(half == 0, tiles[1], tiles[0])
    copies[2].wait()
    for slot, c in enumerate(PACKED):
        for d in range(4):
            packed_ref[slot, 2 * d : 2 * d + 2, :] = momenta_ref[d * 36 + 2 * c : d * 36 + 2 * c + 2, :]


def first_bundle_kernel(place_ref, send_ref, packed_ref, near_ref, sides_ref, out_ref):
    row, _ = iotas()
    odd_time, odd_space = place_ref[0], place_ref[1]
    first = odd_space == 0
    for c in range(12):
        ahead = sides_ref[odd_time, 1, odd_space, c]
        ahead_other = sides_ref[odd_time, 1, 1 - odd_space, c]
        behind_other = sides_ref[1 - odd_time, 0, 1 - odd_space, c]
        partner = near_ref[1 - odd_space, c]
        out_ref[c] = send_ref[c]
        out_ref[12 + c] = jnp.where(row < 2, roll(ahead_other, -2, 0), ahead)
        out_ref[24 + c] = sides_ref[1 - odd_time, 0, odd_space, c]
        out_ref[36 + c] = jnp.where(first & (row // 2 == 1), roll(behind_other, 2, 0), partner)
    for c in range(8):
        out_ref[48 + c] = packed_ref[c]
    for c in range(24):
        out_ref[56 + c] = send_ref[12 + c]
        out_ref[80 + c] = near_ref[1 - odd_space, 12 + c]


def first_kernel(
    place_ref, own_ref, packed_ref, near_ref, sides_ref, across_ref,
    halo_ref, send_ref, far_packed_ref, forward, work, far_own, far_halo,
):
    row, _ = iotas()
    odd_time, odd_space = place_ref[0], place_ref[1]
    first = odd_space == 0
    x_row = row // 2 == 1

    def ahead(c):
        return sides_ref[odd_time, 1, odd_space, c]

    def behind(c):
        return sides_ref[1 - odd_time, 0, odd_space, c]

    def ahead_other(c):
        return sides_ref[odd_time, 1, 1 - odd_space, c]

    def behind_other(c):
        return sides_ref[1 - odd_time, 0, 1 - odd_space, c]

    def near(c):
        return near_ref[1 - odd_space, c]

    def far(group, c):
        return across_ref[odd_space, group * 12 + c]

    def own(c):
        return own_ref[c]

    def put(ref, lead, entry):
        for c, tile in enumerate(completed(entry)):
            ref[lead + (c,)] = tile

    put(halo_ref, (0,), lambda c: jnp.where(row < 2, roll(jnp.where(first, far(1, c), ahead_other(c)), -2, 0), ahead(c)))
    put(halo_ref, (1,), behind)
    put(
        halo_ref,
        (2,),
        lambda c: jnp.where(
            x_row,
            roll(jnp.where(first, behind_other(c), far(2, c)), 2, 0),
            jnp.where(first, near(c), far(0, c)),
        ),
    )
    put(halo_ref, (3,), lambda c: jnp.where(first, far(0, c), near(c)))
    put(far_own, (), lambda c: far(0, c))
    put(far_halo, (0,), lambda c: jnp.where((row < 2) & (odd_space == 1), roll(ahead(c), -2, 0), far(1, c)))
    put(far_halo, (1,), lambda c: far(2, c))
    put(far_halo, (2,), lambda c: jnp.where(first, jnp.where(x_row, roll(behind(c), 2, 0), own(c)), far(3, c)))
    put(far_halo, (3,), lambda c: jnp.where(first, far(3, c), own(c)))
    kick = force(lambda c: far_own[c], lambda h, c: far_halo[h, c], forward, work)
    moved = [far(4, c) - (0.5 * time_step) * kick[c] for c in range(8)]
    for c in range(8):
        far_packed_ref[c] = moved[c]
    for pair in range(4):
        send_ref[8 + pair] = paired(moved[2 * pair], moved[2 * pair + 1])
    kick = force(own, lambda h, c: halo_ref[h, c], forward, work)
    for c in range(8):
        send_ref[c] = packed_ref[c] - (0.5 * time_step) * kick[c]


def drift(own_ref, halo_ref, packed, entry, new_own_ref, new_halo_ref):
    store_matrix(new_own_ref, (), updated(packed, lambda c: own_ref[c]))
    for h in range(4):
        store_matrix(new_halo_ref, (h,), updated(lambda c: entry(h, c), lambda c: halo_ref[h, c]))


def middle_kernel(
    place_ref, own_ref, halo_ref, send_ref, far_packed_ref, near_ref, sides_ref,
    new_own_ref, new_halo_ref, next_ref, forward, work,
):
    row, _ = iotas()
    odd_time, odd_space = place_ref[0], place_ref[1]
    first = odd_space == 0

    def entry(h, c):
        if h == 0:
            main, corner = sides_ref[odd_time, 1, 0, c], unpaired(sides_ref[odd_time, 1, 0, 8 + c // 2], c)
            extra = jnp.where(first, corner, main)
            return jnp.where(row < 2, roll(extra, -2, 0), sides_ref[odd_time, 1, odd_space, c])
        if h == 1:
            return sides_ref[1 - odd_time, 0, odd_space, c]
        near, far = near_ref[1 - odd_space, c], far_packed_ref[c]
        if h == 2:
            main, corner = sides_ref[1 - odd_time, 0, 1, c], unpaired(sides_ref[1 - odd_time, 0, 1, 8 + c // 2], c)
            extra = jnp.where(first, main, corner)
            return jnp.where(row // 2 == 1, roll(extra, 2, 0), jnp.where(first, near, far))
        return jnp.where(first, far, near)

    drift(own_ref, halo_ref, lambda c: send_ref[c], entry, new_own_ref, new_halo_ref)
    kick = force(lambda c: new_own_ref[c], lambda h, c: new_halo_ref[h, c], forward, work)
    for c in range(8):
        next_ref[c] = send_ref[c] - time_step * kick[c]


def last_bundle_kernel(place_ref, own_ref, halo_ref, packed_ref, near_ref, sides_ref, out_ref):
    row, _ = iotas()
    odd_time, odd_space = place_ref[0], place_ref[1]
    first = odd_space == 0

    def corner(c):
        return jnp.where(row < 2, sides_ref[1 - odd_time, 0, odd_space, c], sides_ref[odd_time, 1, odd_space, c])

    for c in range(8):
        out_ref[c] = packed_ref[c]
    for pair in range(4):
        out_ref[8 + pair] = paired(corner(2 * pair), corner(2 * pair + 1))
    even = updated(
        lambda c: jnp.where(first, packed_ref[c], near_ref[1 - odd_space, c]),
        lambda c: jnp.where(first, own_ref[c], halo_ref[3, c]),
    )
    for pair in range(9):
        i, j = pair // 3, pair % 3
        out_ref[12 + pair] = paired(even[i][j][0], even[i][j][1])


def last_drift_kernel(
    place_ref, own_ref, halo_ref, packed_ref, near_ref, sides_ref, across_ref,
    new_own_ref, new_halo_ref, spatial_ref,
):
    row, _ = iotas()
    odd_time, odd_space = place_ref[0], place_ref[1]
    first = odd_space == 0
    x_row = row // 2 == 1

    def entry(h, c):
        if h == 0:
            corner = unpaired(across_ref[odd_space, 8 + c // 2], c)
            extra = jnp.where(first, corner, sides_ref[odd_time, 1, 1 - odd_space, c])
            return jnp.where(row < 2, roll(extra, -2, 0), sides_ref[odd_time, 1, odd_space, c])
        if h == 1:
            return sides_ref[1 - odd_time, 0, odd_space, c]
        near, far = near_ref[1 - odd_space, c], across_ref[odd_space, c]
        if h == 2:
            corner = unpaired(across_ref[odd_space, 8 + c // 2], c)
            extra = jnp.where(first, sides_ref[1 - odd_time, 0, 1 - odd_space, c], corner)
            return jnp.where(x_row, roll(extra, 2, 0), jnp.where(first, near, far))
        return jnp.where(first, far, near)

    drift(own_ref, halo_ref, lambda c: packed_ref[c], entry, new_own_ref, new_halo_ref)
    for c in range(18):
        own, right, left = new_own_ref[c], new_halo_ref[2, c], new_halo_ref[3, c]
        even = unpaired(across_ref[odd_space, 12 + c // 2], c)
        spatial_ref[0, c] = jnp.where(row < 2, roll(left, -2, 0), own)
        spatial_ref[1, c] = jnp.where(
            first,
            jnp.where(row < 2, roll(even, -2, 0), left),
            jnp.where(row < 2, roll(own, -2, 0), jnp.where(x_row, even, right)),
        )


def last_force_kernel(own_ref, halo_ref, packed_ref, links_ref, momenta_ref, forward, work):
    kick = force(lambda c: own_ref[c], lambda h, c: halo_ref[h, c], forward, work)
    final = [packed_ref[c] - (0.5 * time_step) * kick[c] for c in range(8)]
    a0, a1, r01, s01, r02, s02, r12, s12 = final
    zero = jnp.zeros(TILE, F32)
    full = [zero, a0, r01, s01, r02, s02, -r01, s01, zero, a1, r12, s12, -r02, s02, -r12, s12, zero, -(a0 + a1)]
    for c in range(18):
        value = own_ref[c]
        for d in range(4):
            links_ref[d * 36 + 2 * c : d * 36 + 2 * c + 2, :] = value[2 * d : 2 * d + 2, :]
            momenta_ref[d * 36 + 2 * c : d * 36 + 2 * c + 2, :] = full[c][2 * d : 2 * d + 2, :]


def hopping(sides, links, field, ahead, behind, emit):
    row, lane = iotas()
    for side in sides:

        def link(d, c):
            low = jnp.broadcast_to(links(side, c, slice(2 * d, 2 * d + 1)), TILE)
            high = jnp.broadcast_to(links(side, c, slice(2 * d + 1, 2 * d + 2)), TILE)
            return jnp.where(row < 4, low, high)

        totals = {}
        for d in range(4):
            matrix = load_matrix(lambda c: link(d, c))
            for block in range(2):

                def times(vector, dagger):
                    out = []
                    for i in range(3):
                        real, imag = None, None
                        for k in range(3):
                            ar, ai = matrix[k][i] if dagger else matrix[i][k]
                            br, bi = vector[2 * k], vector[2 * k + 1]
                            if dagger:
                                re, im = ar * br + ai * bi, ar * bi - ai * br
                            else:
                                re, im = ar * br - ai * bi, ar * bi + ai * br
                            real = re if real is None else real + re
                            imag = im if imag is None else imag + im
                        out += [real, imag]
                    return out

                tiles = [c * 4 + side * 2 + block for c in range(6)]
                if d == 0:
                    parts = [times([behind(tile) for tile in tiles], True)]
                elif d == 1:
                    parts = [times([ahead(tile) for tile in tiles], False)]
                else:
                    values = [field(tile) for tile in tiles]
                    back = times(values, True)
                    if d == 2:
                        front = times([vector_shift_y(v, 1, lane) for v in values], False)
                        parts = [front, [vector_shift_y(v, -1, lane) for v in back]]
                    else:
                        front = times([shift_z(v, 1, lane) for v in values], False)
                        parts = [front, [shift_z(v, -1, lane) for v in back]]
                for part in parts:
                    for c in range(6):
                        old = totals.get((block, c))
                        totals[block, c] = part[c] if old is None else old + part[c]
        for block in range(2):
            for c in range(6):
                emit(c * 4 + side * 2 + block, totals[block, c] * (-1.0 / 6.0))


def first_hop_kernel(side, place_ref, spatial_ref, field_ref, near_ref, across_ref, *rest):
    odd_space = place_ref[1]
    first = odd_space == 0
    out_ref, far_out_ref = rest[-2:]
    if side == 1:
        for c in range(6):
            for block in range(2):
                tile = c * 4 + block
                out_ref[tile] = rest[0][tile]
                far_out_ref[tile] = rest[1][tile]

    def own(tile):
        return field_ref[12 + tile]

    def near(tile):
        return near_ref[1 - odd_space, 12 + tile]

    def far(tile):
        return across_ref[odd_space, 56 + tile]

    def farther(tile):
        return across_ref[odd_space, 80 + tile]

    def put(ref):
        def emit(tile, value):
            ref[tile] = value

        return emit

    hopping(
        (side,),
        lambda _, c, rows: spatial_ref[0, c, rows, :],
        own,
        lambda tile: jnp.where(first, near(tile), far(tile)),
        lambda tile: jnp.where(first, far(tile), near(tile)),
        put(out_ref),
    )
    hopping(
        (side,),
        lambda _, c, rows: spatial_ref[1, c, rows, :],
        far,
        lambda tile: jnp.where(first, own(tile), farther(tile)),
        lambda tile: jnp.where(first, farther(tile), own(tile)),
        put(far_out_ref),
    )


def second_hop_kernel(place_ref, spatial_ref, other_ref, field_ref, older_ref, near_ref, far_ref, out_ref):
    odd_space = place_ref[1]
    first = odd_space == 0

    def near(tile):
        return near_ref[1 - odd_space, tile]

    def emit(tile, value):
        out_ref[tile] = 2.0 * value - older_ref[12 + tile]

    hopping(
        (0, 1),
        lambda side, c, rows: (other_ref if side else spatial_ref)[0, c, rows, :],
        lambda tile: field_ref[tile],
        lambda tile: jnp.where(first, near(tile), far_ref[tile]),
        lambda tile: jnp.where(first, far_ref[tile], near(tile)),
        emit,
    )


def last_hop_kernel(
    place_ref, coefficients_hbm, spatial_ref, other_ref, field_ref, older_ref, oldest_ref, near_ref, across_ref,
    out_ref, work, coefficients_ref, sem,
):
    copy = pltpu.make_async_copy(coefficients_hbm, coefficients_ref, sem)
    copy.start()
    odd_space, half = place_ref[1], place_ref[2]
    first = odd_space == 0

    def near(tile):
        return near_ref[1 - odd_space, tile]

    def far(tile):
        return across_ref[odd_space, tile]

    def emit(tile, value):
        work[tile] = 2.0 * value - older_ref[tile]

    hopping(
        (0, 1),
        lambda side, c, rows: (other_ref if side else spatial_ref)[0, c, rows, :],
        lambda tile: field_ref[tile],
        lambda tile: jnp.where(first, near(tile), far(tile)),
        lambda tile: jnp.where(first, far(tile), near(tile)),
        emit,
    )
    copy.wait()

    def total(tile):
        value = coefficients_ref[0] * oldest_ref[12 + tile] + coefficients_ref[1] * older_ref[tile]
        return value + coefficients_ref[2] * field_ref[tile] + coefficients_ref[3] * work[tile]

    for c in range(6):
        for block in range(2):
            mine, theirs = total(c * 4 + block), total(c * 4 + 2 + block)
            for h in range(2):
                value = jnp.where(half == h, mine, theirs)
                for side in range(2):
                    out_ref[pl.ds(block * 96 + c * 4 + h * 2 + side, 4, stride=24), :] = value[4 * side : 4 * side + 4, :]


def call(kernel, shapes, inputs, scratch=(), scalars=1, hbm=()):
    def spec(position):
        if position < scalars:
            return pl.BlockSpec(memory_space=pltpu.SMEM)
        return pl.BlockSpec(memory_space=pltpu.HBM if position in hbm else pltpu.VMEM)

    inputs = [
        pltpu.with_memory_space_constraint(value, pltpu.HBM) if position in hbm else value
        for position, value in enumerate(inputs)
    ]
    return pl.pallas_call(
        kernel,
        out_shape=[jax.ShapeDtypeStruct(shape, F32) for shape in shapes],
        in_specs=[spec(position) for position in range(len(inputs))],
        out_specs=[pl.BlockSpec(memory_space=pltpu.VMEM)] * len(shapes),
        scratch_shapes=[pltpu.VMEM(shape, F32) if isinstance(shape, tuple) else shape for shape in scratch],
        compiler_params=pltpu.CompilerParams(vmem_limit_bytes=8 << 20),
        cost_estimate=pl.CostEstimate(flops=4_000_000, bytes_accessed=4_000_000, transcendentals=0),
    )(*inputs)


def pairs(mesh):
    times, spaces = mesh.shape["grp"] * mesh.shape["ta"], mesh.shape["xyz"]

    def at(t, x):
        return (t % times) * spaces + x % spaces

    chip = [[at(t, x), at(t, x + 1)] for t in range(times) for x in range(0, spaces, 2)]
    across = [[at(t, x), at(t, x + 1)] for t in range(times) for x in range(1, spaces, 2)]
    time = [[at(t, x), at(t + 1, x)] for x in range(spaces) for t in range(x % 2, times, 2)]
    return chip, across, time


def body(groups, links, momenta, vectors, coefficients):
    chip, across, time = groups

    def meet(values, which):
        return lax.all_gather(values, AXES, axis_index_groups=which)

    t = lax.axis_index(("grp", "ta"))
    x = lax.axis_index("xyz")
    place = jnp.stack([t % 2, x % 2, lax.axis_index("grp")]).astype(jnp.int32)
    raw = [links.reshape(144, 128), momenta.reshape(144, 128), vectors.reshape(192, 128)]
    own, packed, send = call(
        split_kernel,
        [(18,) + TILE, (8,) + TILE, (36,) + TILE],
        [place] + raw,
        [value.shape for value in raw] + [pltpu.SemaphoreType.DMA((3,))],
        hbm=(1, 2, 3),
    )
    forces = [(3, 18) + TILE, (3, 18) + TILE]

    near = meet(send, chip)
    sides = meet(meet(near[:, :12], time), chip)
    (bundle,) = call(first_bundle_kernel, [(104,) + TILE], [place, send, packed, near, sides])
    far = meet(bundle, across)
    halo, pushed, far_packed = call(
        first_kernel,
        [(4, 18) + TILE, (12,) + TILE, (8,) + TILE],
        [place, own, packed, near, sides, far],
        forces + [(18,) + TILE, (4, 18) + TILE],
    )
    fields, fields_near, fields_far = send, near, far

    near = meet(pushed, chip)
    sides = meet(meet(near, time), chip)
    own, halo, packed = call(
        middle_kernel,
        [(18,) + TILE, (4, 18) + TILE, (8,) + TILE],
        [place, own, halo, pushed, far_packed, near, sides],
        forces,
    )

    near = meet(packed, chip)
    sides = meet(meet(near, time), chip)
    (bundle,) = call(last_bundle_kernel, [(21,) + TILE], [place, own, halo, packed, near, sides])
    own, halo, spatial = call(
        last_drift_kernel,
        [(18,) + TILE, (4, 18) + TILE, (2, 18) + TILE],
        [place, own, halo, packed, near, sides, meet(bundle, across)],
    )

    other = lax.ppermute(spatial, "grp", [(0, 1), (1, 0)])
    vectors_here = [fields, fields_near, fields_far]
    one, far_one = call(
        functools.partial(first_hop_kernel, 0), [(24,) + TILE] * 2, [place, spatial] + vectors_here
    )
    new_links, new_momenta = call(
        last_force_kernel, [(144, 128), (144, 128)], [own, halo, packed], forces, scalars=0
    )
    one, far_one = call(
        functools.partial(first_hop_kernel, 1), [(24,) + TILE] * 2, [place, other] + vectors_here + [one, far_one]
    )
    (two,) = call(
        second_hop_kernel, [(24,) + TILE], [place, spatial, other, one, fields, meet(one, chip), far_one]
    )
    (filtered,) = call(
        last_hop_kernel,
        [(192, 128)],
        [place, coefficients, spatial, other, two, one, fields, meet(two, chip), meet(two, across)],
        [(24,) + TILE, pltpu.SMEM((4,), F32), pltpu.SemaphoreType.DMA],
        hbm=(1,),
    )
    return (
        new_links.reshape(links.shape),
        new_momenta.reshape(momenta.shape),
        filtered.reshape(vectors.shape),
    )


def solution(mesh):
    return jax.shard_map(
        functools.partial(body, pairs(mesh)),
        mesh=mesh,
        in_specs=(
            P(None, None, None, None, ("grp", "ta"), "xyz", None),
            P(None, None, None, None, ("grp", "ta"), "xyz", None),
            P("grp", None, None, None, "ta", "xyz", None),
            P(),
        ),
        out_specs=(
            P(None, None, None, None, ("grp", "ta"), "xyz", None),
            P(None, None, None, None, ("grp", "ta"), "xyz", None),
            P("grp", None, None, None, "ta", "xyz", None),
        ),
        check_vma=False,
    )
```

```python
import functools

import jax
import jax.numpy as jnp
from jax import lax
from jax.experimental import pallas as pl
from jax.experimental.pallas import tpu as pltpu
from jax.sharding import PartitionSpec as P

NZ = 32
NSTEP = 2
NCHEB = 3
coupling = 5.7
time_step = 0.1
taylor_degree = 6

AXES = ("grp", "ta", "xyz")
TILE = (8, 128)
F32 = jnp.float32


def roll(value, shift, axis):
    return pltpu.roll(value, shift % value.shape[axis], axis)


def iotas():
    row = lax.broadcasted_iota(jnp.int32, TILE, 0)
    lane = lax.broadcasted_iota(jnp.int32, TILE, 1)
    return row, lane


def load_matrix(entry):
    return [[(entry((i * 3 + j) * 2), entry((i * 3 + j) * 2 + 1)) for j in range(3)] for i in range(3)]


def product(left, right, left_h=False, right_h=False):
    out = []
    for i in range(3):
        line = []
        for j in range(3):
            real, imag = None, None
            for k in range(3):
                ar, ai = left[k][i] if left_h else left[i][k]
                br, bi = right[j][k] if right_h else right[k][j]
                rr, ii, ri, ir = ar * br, ai * bi, ar * bi, ai * br
                re = rr + ii if left_h != right_h else rr - ii
                if left_h and right_h:
                    im_terms = (-1, ri, ir)
                elif left_h:
                    im_terms = (1, ri, -1, ir)
                elif right_h:
                    im_terms = (1, ir, -1, ri)
                else:
                    im_terms = (1, ri, ir)
                real = re if real is None else real + re
                if len(im_terms) == 4:
                    im = im_terms[1] - im_terms[3]
                    imag = im if imag is None else imag + im
                else:
                    im = im_terms[1] + im_terms[2]
                    if im_terms[0] < 0:
                        imag = -im if imag is None else imag - im
                    else:
                        imag = im if imag is None else imag + im
            line.append((real, imag))
        out.append(line)
    return out


def exponential(packed, scale):
    a0, a1, r01, s01, r02, s02, r12, s12 = [packed(c) * scale for c in range(8)]
    a2 = -(a0 + a1)
    h01, h02, h12 = (s01, -r01), (s02, -r02), (s12, -r12)
    n01, n02, n12 = (s01 * s01 + r01 * r01, s02 * s02 + r02 * r02, s12 * s12 + r12 * r12)
    d0, d1, d2 = a0 * a0, a1 * a1, a2 * a2
    p = 0.5 * (d0 + d1 + d2) + (n01 + n02 + n12)

    def cmul(x, y):
        return (x[0] * y[0] - x[1] * y[1], x[0] * y[1] + x[1] * y[0])

    def cmul_conj(x, y):
        return (x[0] * y[0] + x[1] * y[1], x[1] * y[0] - x[0] * y[1])

    m = cmul(h01, h12)
    q = a0 * a1 * a2 + 2.0 * (m[0] * h02[0] + m[1] * h02[1]) - a0 * n12 - a1 * n02 - a2 * n01
    k01 = cmul_conj(h02, h12)
    k12 = cmul_conj(h02, h01)
    g01 = (k01[0] - a2 * h01[0], k01[1] - a2 * h01[1])
    g02 = (m[0] - a1 * h02[0], m[1] - a1 * h02[1])
    g12 = (k12[0] - a0 * h12[0], k12[1] - a0 * h12[1])
    g00, g11, g22 = d0 + n01 + n02, d1 + n01 + n12, d2 + n02 + n12
    assert taylor_degree == 6
    c2 = -1.0 / 30.0
    f0 = (None, (c2 / 4.0) * q)
    f1 = (None, 0.25 + (c2 / 4.0) * p)
    f2r = -1.0 / 20.0
    t0 = f2r * q
    u0r, u0i = 1.0 + f2r * p, f0[1]
    w = f1[1]
    f0 = (1.0, t0 * (1.0 / 3.0))
    f1 = (-u0i * (1.0 / 3.0), u0r * (1.0 / 3.0))
    f2 = (-w * (1.0 / 3.0), None)
    t0 = f2[0] * q
    u0r, u0i = 1.0 + f2[0] * p, f0[1]
    f0 = (1.0, t0 * 0.5)
    f2 = (-f1[1] * 0.5, f1[0] * 0.5)
    f1 = (-u0i * 0.5, u0r * 0.5)
    f0, f1, f2 = (
        (1.0 - f2[1] * q, f2[0] * q),
        (-(f0[1] + f2[1] * p), 1.0 + f2[0] * p),
        (-f1[1], f1[0]),
    )

    def pair(h, g):
        rr = f1[0] * h[0] + f2[0] * g[0]
        ii = f1[1] * h[1] + f2[1] * g[1]
        ri = f1[0] * h[1] + f2[0] * g[1]
        ir = f1[1] * h[0] + f2[1] * g[0]
        return (rr - ii, ri + ir), (rr + ii, ir - ri)

    def diag(a, g):
        return (f0[0] + f1[0] * a + f2[0] * g, f0[1] + f1[1] * a + f2[1] * g)

    e01, e10 = pair(h01, g01)
    e02, e20 = pair(h02, g02)
    e12, e21 = pair(h12, g12)
    return [
        [diag(a0, g00), e01, e02],
        [e10, diag(a1, g11), e12],
        [e20, e21, diag(a2, g22)],
    ]


def store_matrix(ref, lead, matrix):
    for i in range(3):
        for j in range(3):
            for part in range(2):
                ref[lead + ((i * 3 + j) * 2 + part,)] = matrix[i][j][part]


def updated(packed, entry):
    return product(exponential(packed, time_step), load_matrix(entry))


def link_shift_y(value, amount, row, lane):
    if amount == 1:
        rolled = roll(value, -NZ, 1)
        inside = lane < 128 - NZ
    else:
        rolled = roll(value, NZ, 1)
        inside = lane >= NZ
    other = jnp.where(row % 2 == 1, roll(rolled, 1, 0), roll(rolled, -1, 0))
    return jnp.where(inside, rolled, other)


def vector_shift_y(value, amount, lane):
    if amount == 1:
        rolled = roll(value, -NZ, 1)
        inside = lane < 128 - NZ
    else:
        rolled = roll(value, NZ, 1)
        inside = lane >= NZ
    return jnp.where(inside, rolled, roll(rolled, 4, 0))


def shift_z(value, amount, lane):
    if amount == 1:
        return jnp.where(lane % NZ == NZ - 1, roll(value, NZ - 1, 1), roll(value, -1, 1))
    return jnp.where(lane % NZ == 0, roll(value, -(NZ - 1), 1), roll(value, 1, 1))


def force(own, halo, forward, work):
    row, lane = iotas()
    direction = row // 2
    is_dir = [direction == d for d in range(4)]
    for c in range(18):
        value = own(c)
        ahead = [
            halo(0, c),
            halo(2, c),
            link_shift_y(value, 1, row, lane),
            shift_z(value, 1, lane),
        ]
        for k in range(1, 4):
            forward[k - 1, c] = jnp.where(
                is_dir[0],
                ahead[k % 4],
                jnp.where(
                    is_dir[1], ahead[(1 + k) % 4], jnp.where(is_dir[2], ahead[(2 + k) % 4], ahead[(3 + k) % 4])
                ),
            )

    def turned(value, k):
        return roll(value, -2 * k, 0)

    def base(c):
        return jnp.where(is_dir[0], halo(1, c), jnp.where(is_dir[1], halo(3, c), own(c)))

    def corner_ahead(k, c):
        plain = turned(forward[3 - k, c], k)
        if k == 1:
            moved = turned(shift_z(turned(base(c), 2), 1, lane), -1)
            return jnp.where(is_dir[3], moved, jnp.where(is_dir[0], halo(0, c), plain))
        start = turned(base(c), 2)
        if k == 2:
            return jnp.where(
                is_dir[2],
                link_shift_y(start, 1, row, lane),
                jnp.where(is_dir[3], shift_z(start, 1, lane), plain),
            )
        moved = turned(link_shift_y(start, 1, row, lane), 1)
        return jnp.where(is_dir[1], halo(2, c), jnp.where(is_dir[2], moved, plain))

    def here(k, c):
        value = own(c)
        time_row, space_row = {1: (3, 0), 2: (2, 3), 3: (1, 2)}[k]
        return jnp.where(is_dir[time_row], halo(1, c), jnp.where(is_dir[space_row], halo(3, c), value))

    for k in range(1, 4):
        up = product(
            load_matrix(lambda c: turned(forward[3 - k, c], k)),
            load_matrix(lambda c: forward[k - 1, c]),
            right_h=True,
        )
        up = product(up, load_matrix(lambda c: turned(own(c), k)), right_h=True)
        low = product(load_matrix(lambda c: here(k, c)), load_matrix(lambda c: corner_ahead(k, c)))
        low = product(low, load_matrix(lambda c: turned(base(c), k)), left_h=True)
        direct = {1: is_dir[0] | is_dir[3], 2: is_dir[2] | is_dir[3], 3: is_dir[1] | is_dir[2]}[k]
        for c in range(18):
            i, j, part = c // 6, (c // 2) % 3, c % 2
            staple, down = up[i][j][part], low[i][j][part]
            staple = staple + jnp.where(direct, down, 0.0)
            if k == 1:
                work[0, c], work[1, c], work[2, c] = staple, down, down
            else:
                y_row, z_row = {2: (0, 1), 3: (3, 0)}[k]
                work[0, c] = work[0, c] + staple
                work[1, c] = jnp.where(is_dir[y_row], down, work[1, c])
                work[2, c] = jnp.where(is_dir[z_row], down, work[2, c])

    def staples(c):
        y_part = jnp.where(is_dir[2], 0.0, link_shift_y(work[1, c], -1, row, lane))
        z_part = jnp.where(is_dir[3], 0.0, shift_z(work[2, c], -1, lane))
        return work[0, c] + y_part + z_part

    total = product(load_matrix(own), load_matrix(staples))
    mean = (total[0][0][1] + total[1][1][1] + total[2][2][1]) * (1.0 / 3.0)
    factor = coupling / 3.0
    out = [(total[0][0][1] - mean) * factor, (total[1][1][1] - mean) * factor]
    for i, j in ((0, 1), (0, 2), (1, 2)):
        out.append((total[i][j][0] - total[j][i][0]) * (0.5 * factor))
        out.append((total[i][j][1] + total[j][i][1]) * (0.5 * factor))
    return out


def completed(entry):
    tiles = [entry(c) for c in range(12)]
    a = [(tiles[2 * j], tiles[2 * j + 1]) for j in range(3)]
    b = [(tiles[6 + 2 * j], tiles[7 + 2 * j]) for j in range(3)]
    for j in range(3):
        p, q = (j + 1) % 3, (j + 2) % 3
        real = (a[p][0] * b[q][0] - a[p][1] * b[q][1]) - (a[q][0] * b[p][0] - a[q][1] * b[p][1])
        imag = (a[p][0] * b[q][1] + a[p][1] * b[q][0]) - (a[q][0] * b[p][1] + a[q][1] * b[p][0])
        tiles += [real, -imag]
    return tiles


def paired(even, odd):
    row, _ = iotas()
    return jnp.where(row < 4, even, roll(odd, 4, 0))


def unpaired(tile, c):
    return roll(tile, 4, 0) if c % 2 else tile


PACKED = (1, 9, 2, 3, 4, 5, 10, 11)


def split_kernel(place, links_hbm, momenta_hbm, vectors_hbm, own_ref, packed_ref, send_ref, links_ref, momenta_ref, vectors_ref, sems):
    half = place[2]
    copies = [
        pltpu.make_async_copy(source, target, sems.at[i])
        for i, (source, target) in enumerate(
            ((links_hbm, links_ref), (vectors_hbm, vectors_ref), (momenta_hbm, momenta_ref))
        )
    ]
    for copy in copies:
        copy.start()
    copies[0].wait()
    for c in range(18):
        for d in range(4):
            value = links_ref[d * 36 + 2 * c : d * 36 + 2 * c + 2, :]
            own_ref[c, 2 * d : 2 * d + 2, :] = value
            if c < 12:
                send_ref[c, 2 * d : 2 * d + 2, :] = value
    copies[1].wait()
    for c in range(6):
        for block in range(2):
            tiles = []
            for h in range(2):
                parts = [
                    vectors_ref[pl.ds(block * 96 + c * 4 + h * 2 + side, 4, stride=24), :] for side in range(2)
                ]
                tiles.append(jnp.concatenate(parts, axis=0))
            send_ref[12 + c * 4 + block] = jnp.where(half == 0, tiles[0], tiles[1])
            send_ref[12 + c * 4 + 2 + block] = jnp.where(half == 0, tiles[1], tiles[0])
    copies[2].wait()
    for slot, c in enumerate(PACKED):
        for d in range(4):
            packed_ref[slot, 2 * d : 2 * d + 2, :] = momenta_ref[d * 36 + 2 * c : d * 36 + 2 * c + 2, :]


def first_bundle_kernel(place, send_ref, packed_ref, near_ref, sides_ref, out_ref):
    row, _ = iotas()
    odd_time, odd_space = place[0], place[1]
    first = odd_space == 0
    for c in range(12):
        ahead = sides_ref[odd_time, 1, odd_space, c]
        ahead_other = sides_ref[odd_time, 1, 1 - odd_space, c]
        behind_other = sides_ref[1 - odd_time, 0, 1 - odd_space, c]
        partner = near_ref[1 - odd_space, c]
        out_ref[c] = send_ref[c]
        out_ref[12 + c] = jnp.where(row < 2, roll(ahead_other, -2, 0), ahead)
        out_ref[24 + c] = sides_ref[1 - odd_time, 0, odd_space, c]
        out_ref[36 + c] = jnp.where(first & (row // 2 == 1), roll(behind_other, 2, 0), partner)
    for c in range(8):
        out_ref[48 + c] = packed_ref[c]
    for c in range(24):
        out_ref[56 + c] = send_ref[12 + c]
        out_ref[80 + c] = near_ref[1 - odd_space, 12 + c]


def first_kernel(
    place, own_ref, packed_ref, near_ref, sides_ref, across_ref,
    halo_ref, send_ref, far_packed_ref, forward, work, far_own, far_halo,
):
    row, _ = iotas()
    odd_time, odd_space = place[0], place[1]
    first = odd_space == 0
    x_row = row // 2 == 1

    def ahead(c):
        return sides_ref[odd_time, 1, odd_space, c]

    def behind(c):
        return sides_ref[1 - odd_time, 0, odd_space, c]

    def ahead_other(c):
        return sides_ref[odd_time, 1, 1 - odd_space, c]

    def behind_other(c):
        return sides_ref[1 - odd_time, 0, 1 - odd_space, c]

    def near(c):
        return near_ref[1 - odd_space, c]

    def far(group, c):
        return across_ref[odd_space, group * 12 + c]

    def own(c):
        return own_ref[c]

    def put(ref, lead, entry):
        for c, tile in enumerate(completed(entry)):
            ref[lead + (c,)] = tile

    put(halo_ref, (0,), lambda c: jnp.where(row < 2, roll(jnp.where(first, far(1, c), ahead_other(c)), -2, 0), ahead(c)))
    put(halo_ref, (1,), behind)
    put(
        halo_ref,
        (2,),
        lambda c: jnp.where(
            x_row,
            roll(jnp.where(first, behind_other(c), far(2, c)), 2, 0),
            jnp.where(first, near(c), far(0, c)),
        ),
    )
    put(halo_ref, (3,), lambda c: jnp.where(first, far(0, c), near(c)))
    put(far_own, (), lambda c: far(0, c))
    put(far_halo, (0,), lambda c: jnp.where((row < 2) & (odd_space == 1), roll(ahead(c), -2, 0), far(1, c)))
    put(far_halo, (1,), lambda c: far(2, c))
    put(far_halo, (2,), lambda c: jnp.where(first, jnp.where(x_row, roll(behind(c), 2, 0), own(c)), far(3, c)))
    put(far_halo, (3,), lambda c: jnp.where(first, far(3, c), own(c)))
    kick = force(lambda c: far_own[c], lambda h, c: far_halo[h, c], forward, work)
    moved = [far(4, c) - (0.5 * time_step) * kick[c] for c in range(8)]
    for c in range(8):
        far_packed_ref[c] = moved[c]
    for pair in range(4):
        send_ref[8 + pair] = paired(moved[2 * pair], moved[2 * pair + 1])
    kick = force(own, lambda h, c: halo_ref[h, c], forward, work)
    for c in range(8):
        send_ref[c] = packed_ref[c] - (0.5 * time_step) * kick[c]


def drift(own_ref, halo_ref, packed, entry, new_own_ref, new_halo_ref):
    store_matrix(new_own_ref, (), updated(packed, lambda c: own_ref[c]))
    for h in range(4):
        store_matrix(new_halo_ref, (h,), updated(lambda c: entry(h, c), lambda c: halo_ref[h, c]))


def middle_kernel(
    place, own_ref, halo_ref, send_ref, far_packed_ref, near_ref, sides_ref,
    new_own_ref, new_halo_ref, next_ref, forward, work,
):
    row, _ = iotas()
    odd_time, odd_space = place[0], place[1]
    first = odd_space == 0

    def entry(h, c):
        if h == 0:
            main, corner = sides_ref[odd_time, 1, 0, c], unpaired(sides_ref[odd_time, 1, 0, 8 + c // 2], c)
            extra = jnp.where(first, corner, main)
            return jnp.where(row < 2, roll(extra, -2, 0), sides_ref[odd_time, 1, odd_space, c])
        if h == 1:
            return sides_ref[1 - odd_time, 0, odd_space, c]
        near, far = near_ref[1 - odd_space, c], far_packed_ref[c]
        if h == 2:
            main, corner = sides_ref[1 - odd_time, 0, 1, c], unpaired(sides_ref[1 - odd_time, 0, 1, 8 + c // 2], c)
            extra = jnp.where(first, main, corner)
            return jnp.where(row // 2 == 1, roll(extra, 2, 0), jnp.where(first, near, far))
        return jnp.where(first, far, near)

    drift(own_ref, halo_ref, lambda c: send_ref[c], entry, new_own_ref, new_halo_ref)
    kick = force(lambda c: new_own_ref[c], lambda h, c: new_halo_ref[h, c], forward, work)
    for c in range(8):
        next_ref[c] = send_ref[c] - time_step * kick[c]


def last_bundle_kernel(place, own_ref, halo_ref, packed_ref, near_ref, sides_ref, out_ref):
    row, _ = iotas()
    odd_time, odd_space = place[0], place[1]
    first = odd_space == 0

    def corner(c):
        return jnp.where(row < 2, sides_ref[1 - odd_time, 0, odd_space, c], sides_ref[odd_time, 1, odd_space, c])

    for c in range(8):
        out_ref[c] = packed_ref[c]
    for pair in range(4):
        out_ref[8 + pair] = paired(corner(2 * pair), corner(2 * pair + 1))
    even = updated(
        lambda c: jnp.where(first, packed_ref[c], near_ref[1 - odd_space, c]),
        lambda c: jnp.where(first, own_ref[c], halo_ref[3, c]),
    )
    for pair in range(9):
        i, j = pair // 3, pair % 3
        out_ref[12 + pair] = paired(even[i][j][0], even[i][j][1])


def last_drift_kernel(
    place, own_ref, halo_ref, packed_ref, near_ref, sides_ref, across_ref,
    new_own_ref, new_halo_ref, spatial_ref,
):
    row, _ = iotas()
    odd_time, odd_space = place[0], place[1]
    first = odd_space == 0
    x_row = row // 2 == 1

    def entry(h, c):
        if h == 0:
            corner = unpaired(across_ref[odd_space, 8 + c // 2], c)
            extra = jnp.where(first, corner, sides_ref[odd_time, 1, 1 - odd_space, c])
            return jnp.where(row < 2, roll(extra, -2, 0), sides_ref[odd_time, 1, odd_space, c])
        if h == 1:
            return sides_ref[1 - odd_time, 0, odd_space, c]
        near, far = near_ref[1 - odd_space, c], across_ref[odd_space, c]
        if h == 2:
            corner = unpaired(across_ref[odd_space, 8 + c // 2], c)
            extra = jnp.where(first, sides_ref[1 - odd_time, 0, 1 - odd_space, c], corner)
            return jnp.where(x_row, roll(extra, 2, 0), jnp.where(first, near, far))
        return jnp.where(first, far, near)

    drift(own_ref, halo_ref, lambda c: packed_ref[c], entry, new_own_ref, new_halo_ref)
    for c in range(18):
        own, right, left = new_own_ref[c], new_halo_ref[2, c], new_halo_ref[3, c]
        even = unpaired(across_ref[odd_space, 12 + c // 2], c)
        spatial_ref[0, c] = jnp.where(row < 2, roll(left, -2, 0), own)
        spatial_ref[1, c] = jnp.where(
            first,
            jnp.where(row < 2, roll(even, -2, 0), left),
            jnp.where(row < 2, roll(own, -2, 0), jnp.where(x_row, even, right)),
        )


def last_force_kernel(own_ref, halo_ref, packed_ref, links_ref, momenta_ref, forward, work):
    kick = force(lambda c: own_ref[c], lambda h, c: halo_ref[h, c], forward, work)
    final = [packed_ref[c] - (0.5 * time_step) * kick[c] for c in range(8)]
    a0, a1, r01, s01, r02, s02, r12, s12 = final
    zero = jnp.zeros(TILE, F32)
    full = [zero, a0, r01, s01, r02, s02, -r01, s01, zero, a1, r12, s12, -r02, s02, -r12, s12, zero, -(a0 + a1)]
    for c in range(18):
        value = own_ref[c]
        for d in range(4):
            links_ref[d * 36 + 2 * c : d * 36 + 2 * c + 2, :] = value[2 * d : 2 * d + 2, :]
            momenta_ref[d * 36 + 2 * c : d * 36 + 2 * c + 2, :] = full[c][2 * d : 2 * d + 2, :]


def hopping(sides, links, field, ahead, behind, emit):
    row, lane = iotas()
    for side in sides:

        def link(d, c):
            low = jnp.broadcast_to(links(side, c, slice(2 * d, 2 * d + 1)), TILE)
            high = jnp.broadcast_to(links(side, c, slice(2 * d + 1, 2 * d + 2)), TILE)
            return jnp.where(row < 4, low, high)

        totals = {}
        for d in range(4):
            matrix = load_matrix(lambda c: link(d, c))
            for block in range(2):

                def times(vector, dagger):
                    out = []
                    for i in range(3):
                        real, imag = None, None
                        for k in range(3):
                            ar, ai = matrix[k][i] if dagger else matrix[i][k]
                            br, bi = vector[2 * k], vector[2 * k + 1]
                            if dagger:
                                re, im = ar * br + ai * bi, ar * bi - ai * br
                            else:
                                re, im = ar * br - ai * bi, ar * bi + ai * br
                            real = re if real is None else real + re
                            imag = im if imag is None else imag + im
                        out += [real, imag]
                    return out

                tiles = [c * 4 + side * 2 + block for c in range(6)]
                if d == 0:
                    parts = [times([behind(tile) for tile in tiles], True)]
                elif d == 1:
                    parts = [times([ahead(tile) for tile in tiles], False)]
                else:
                    values = [field(tile) for tile in tiles]
                    back = times(values, True)
                    if d == 2:
                        front = times([vector_shift_y(v, 1, lane) for v in values], False)
                        parts = [front, [vector_shift_y(v, -1, lane) for v in back]]
                    else:
                        front = times([shift_z(v, 1, lane) for v in values], False)
                        parts = [front, [shift_z(v, -1, lane) for v in back]]
                for part in parts:
                    for c in range(6):
                        old = totals.get((block, c))
                        totals[block, c] = part[c] if old is None else old + part[c]
        for block in range(2):
            for c in range(6):
                emit(c * 4 + side * 2 + block, totals[block, c] * (-1.0 / 6.0))


def first_hop_kernel(side, place, spatial_ref, field_ref, near_ref, across_ref, *rest):
    odd_space = place[1]
    first = odd_space == 0
    out_ref, far_out_ref = rest[-2:]
    if side == 1:
        for c in range(6):
            for block in range(2):
                tile = c * 4 + block
                out_ref[tile] = rest[0][tile]
                far_out_ref[tile] = rest[1][tile]

    def own(tile):
        return field_ref[12 + tile]

    def near(tile):
        return near_ref[1 - odd_space, 12 + tile]

    def far(tile):
        return across_ref[odd_space, 56 + tile]

    def farther(tile):
        return across_ref[odd_space, 80 + tile]

    def put(ref):
        def emit(tile, value):
            ref[tile] = value

        return emit

    hopping(
        (side,),
        lambda _, c, rows: spatial_ref[0, c, rows, :],
        own,
        lambda tile: jnp.where(first, near(tile), far(tile)),
        lambda tile: jnp.where(first, far(tile), near(tile)),
        put(out_ref),
    )
    hopping(
        (side,),
        lambda _, c, rows: spatial_ref[1, c, rows, :],
        far,
        lambda tile: jnp.where(first, own(tile), farther(tile)),
        lambda tile: jnp.where(first, farther(tile), own(tile)),
        put(far_out_ref),
    )


def second_hop_kernel(place, spatial_ref, other_ref, field_ref, older_ref, near_ref, far_ref, out_ref):
    odd_space = place[1]
    first = odd_space == 0

    def near(tile):
        return near_ref[1 - odd_space, tile]

    def emit(tile, value):
        out_ref[tile] = 2.0 * value - older_ref[12 + tile]

    hopping(
        (0, 1),
        lambda side, c, rows: (other_ref if side else spatial_ref)[0, c, rows, :],
        lambda tile: field_ref[tile],
        lambda tile: jnp.where(first, near(tile), far_ref[tile]),
        lambda tile: jnp.where(first, far_ref[tile], near(tile)),
        emit,
    )


def last_hop_kernel(
    place, coefficients_hbm, spatial_ref, other_ref, field_ref, older_ref, oldest_ref, near_ref, across_ref,
    out_ref, work, coefficients_ref, sem,
):
    copy = pltpu.make_async_copy(coefficients_hbm, coefficients_ref, sem)
    copy.start()
    odd_space, half = place[1], place[2]
    first = odd_space == 0

    def near(tile):
        return near_ref[1 - odd_space, tile]

    def far(tile):
        return across_ref[odd_space, tile]

    def emit(tile, value):
        work[tile] = 2.0 * value - older_ref[tile]

    hopping(
        (0, 1),
        lambda side, c, rows: (other_ref if side else spatial_ref)[0, c, rows, :],
        lambda tile: field_ref[tile],
        lambda tile: jnp.where(first, near(tile), far(tile)),
        lambda tile: jnp.where(first, far(tile), near(tile)),
        emit,
    )
    copy.wait()

    def total(tile):
        value = coefficients_ref[0] * oldest_ref[12 + tile] + coefficients_ref[1] * older_ref[tile]
        return value + coefficients_ref[2] * field_ref[tile] + coefficients_ref[3] * work[tile]

    for c in range(6):
        for block in range(2):
            mine, theirs = total(c * 4 + block), total(c * 4 + 2 + block)
            for h in range(2):
                value = jnp.where(half == h, mine, theirs)
                for side in range(2):
                    out_ref[pl.ds(block * 96 + c * 4 + h * 2 + side, 4, stride=24), :] = value[4 * side : 4 * side + 4, :]


def here():
    half = lax.axis_index("grp")
    t = half * lax.axis_size("ta") + lax.axis_index("ta")
    return lax.rem(t, 2), lax.rem(lax.axis_index("xyz"), 2), half


def call(kernel, shapes, inputs, scratch=(), placed=True, hbm=()):
    def run(*refs):
        return kernel(here(), *refs) if placed else kernel(*refs)

    inputs = [
        pltpu.with_memory_space_constraint(value, pltpu.HBM) if position in hbm else value
        for position, value in enumerate(inputs)
    ]
    return pl.pallas_call(
        run,
        out_shape=[jax.ShapeDtypeStruct(shape, F32) for shape in shapes],
        in_specs=[
            pl.BlockSpec(memory_space=pltpu.HBM if position in hbm else pltpu.VMEM) for position in range(len(inputs))
        ],
        out_specs=[pl.BlockSpec(memory_space=pltpu.VMEM)] * len(shapes),
        scratch_shapes=[pltpu.VMEM(shape, F32) if isinstance(shape, tuple) else shape for shape in scratch],
        compiler_params=pltpu.CompilerParams(vmem_limit_bytes=8 << 20),
        cost_estimate=pl.CostEstimate(flops=4_000_000, bytes_accessed=4_000_000, transcendentals=0),
    )(*inputs)


def pairs(mesh):
    times, spaces = mesh.shape["grp"] * mesh.shape["ta"], mesh.shape["xyz"]

    def at(t, x):
        return (t % times) * spaces + x % spaces

    chip = [[at(t, x), at(t, x + 1)] for t in range(times) for x in range(0, spaces, 2)]
    across = [[at(t, x), at(t, x + 1)] for t in range(times) for x in range(1, spaces, 2)]
    time = [[at(t, x), at(t + 1, x)] for x in range(spaces) for t in range(x % 2, times, 2)]
    return chip, across, time


def body(groups, links, momenta, vectors, coefficients):
    chip, across, time = groups

    def meet(values, which):
        return lax.all_gather(values, AXES, axis_index_groups=which)

    raw = [links.reshape(144, 128), momenta.reshape(144, 128), vectors.reshape(192, 128)]
    own, packed, send = call(
        split_kernel,
        [(18,) + TILE, (8,) + TILE, (36,) + TILE],
        raw,
        [value.shape for value in raw] + [pltpu.SemaphoreType.DMA((3,))],
        hbm=(0, 1, 2),
    )
    forces = [(3, 18) + TILE, (3, 18) + TILE]

    near = meet(send, chip)
    sides = meet(meet(near[:, :12], time), chip)
    (bundle,) = call(first_bundle_kernel, [(104,) + TILE], [send, packed, near, sides])
    far = meet(bundle, across)
    halo, pushed, far_packed = call(
        first_kernel,
        [(4, 18) + TILE, (12,) + TILE, (8,) + TILE],
        [own, packed, near, sides, far],
        forces + [(18,) + TILE, (4, 18) + TILE],
    )
    fields, fields_near, fields_far = send, near, far

    near = meet(pushed, chip)
    sides = meet(meet(near, time), chip)
    own, halo, packed = call(
        middle_kernel,
        [(18,) + TILE, (4, 18) + TILE, (8,) + TILE],
        [own, halo, pushed, far_packed, near, sides],
        forces,
    )

    near = meet(packed, chip)
    sides = meet(meet(near, time), chip)
    (bundle,) = call(last_bundle_kernel, [(21,) + TILE], [own, halo, packed, near, sides])
    own, halo, spatial = call(
        last_drift_kernel,
        [(18,) + TILE, (4, 18) + TILE, (2, 18) + TILE],
        [own, halo, packed, near, sides, meet(bundle, across)],
    )

    other = lax.ppermute(spatial, "grp", [(0, 1), (1, 0)])
    vectors_here = [fields, fields_near, fields_far]
    one, far_one = call(
        functools.partial(first_hop_kernel, 0), [(24,) + TILE] * 2, [spatial] + vectors_here
    )
    new_links, new_momenta = call(
        last_force_kernel, [(144, 128), (144, 128)], [own, halo, packed], forces, placed=False
    )
    one, far_one = call(
        functools.partial(first_hop_kernel, 1), [(24,) + TILE] * 2, [other] + vectors_here + [one, far_one]
    )
    (two,) = call(
        second_hop_kernel, [(24,) + TILE], [spatial, other, one, fields, meet(one, chip), far_one]
    )
    (filtered,) = call(
        last_hop_kernel,
        [(192, 128)],
        [coefficients, spatial, other, two, one, fields, meet(two, chip), meet(two, across)],
        [(24,) + TILE, pltpu.SMEM((4,), F32), pltpu.SemaphoreType.DMA],
        hbm=(0,),
    )
    return (
        new_links.reshape(links.shape),
        new_momenta.reshape(momenta.shape),
        filtered.reshape(vectors.shape),
    )


def solution(mesh):
    return jax.shard_map(
        functools.partial(body, pairs(mesh)),
        mesh=mesh,
        in_specs=(
            P(None, None, None, None, ("grp", "ta"), "xyz", None),
            P(None, None, None, None, ("grp", "ta"), "xyz", None),
            P("grp", None, None, None, "ta", "xyz", None),
            P(),
        ),
        out_specs=(
            P(None, None, None, None, ("grp", "ta"), "xyz", None),
            P(None, None, None, None, ("grp", "ta"), "xyz", None),
            P("grp", None, None, None, "ta", "xyz", None),
        ),
        check_vma=False,
    )
```
